512 devices in a mesh: mem: 16 (over z, core), head: 8 (over y), span: 4 (over x).
Axes of the slice: x: 4, y: 8, z: 8, core: 2. Of those that a mesh axis runs over, the one named last changes fastest.
Arguments:
- query: bfloat16 [4, 2048, 8, 8, 128], P('span', 'mem', 'head'), may hold values from -6 to 6
- new_keys: bfloat16 [4, 2048, 8, 128], P('span', 'mem', 'head'), may hold values from -6 to 6
- new_values: bfloat16 [4, 2048, 8, 128], P('span', 'mem', 'head'), may hold values from -5 to 5
- memory_keys: bfloat16 [512, 128, 8, 128], P('mem', None, 'head'), may hold values from -5 to 5
- memory_values: bfloat16 [512, 128, 8, 128], P('mem', None, 'head'), may hold values from -5 to 5
- retrieved: int32 [4, 8, 16], P('span', 'head'), may hold values from 0 to 511, as said below
Outputs:
- attended: bfloat16 [4, 2048, 8192], P('span', ('mem', 'head'))
The draws below stay inside these ranges and needn't reach their ends.
Inputs may be any that keep to these rules, and one draw needn't show every extreme that they name: Each list retrieved[b, h, :] names 16 different units. The units o * 32 to (o + 1) * 32 - 1 appear at most 3 times in one list, and in every list some o has exactly 3.
All inputs are finite; a program needn't handle non-finite values.
Results may differ from the reference program's by a relative error of at most 0.005.
Values may be sent and summed in bfloat16 or wider, within the bound.
A program may use at most 64 MiB of HBM per device.

```python
import math
import jax
import jax.numpy as jnp
from jax import lax

KVH = 8
HD = 128
UNIT = 128
TOPK = 16
UNITS_DEV = 32
QPK = 8
NBLOCKS = 4
BLOCK_LEN = 2048
UNITS = 512
CAP = 3
N_MEM = 16


def draw_query(key, part):
    shape = (NBLOCKS, BLOCK_LEN, KVH, QPK, HD)
    base_key = jax.random.fold_in(key, 11)
    values = 2.0 * jax.random.truncated_normal(base_key, -3.0, 3.0, shape)
    return values.astype(jnp.bfloat16)


def draw_new_keys(key, part):
    shape = (NBLOCKS, BLOCK_LEN, KVH, HD)
    base_key = jax.random.fold_in(key, 13)
    values = jax.random.truncated_normal(base_key, -4.0, 4.0, shape)
    return values.astype(jnp.bfloat16)


def draw_retrieved(key, part):
    pair_count = N_MEM * CAP
    owner_of = jnp.arange(pair_count) // CAP
    slot_of = jnp.arange(pair_count) % CAP

    def unit_order(unit_key):
        return jax.random.permutation(unit_key, UNITS_DEV)[:CAP]

    def one_list(list_key):
        hot_key, order_key, unit_key = jax.random.split(list_key, 3)
        hot_owner = jax.random.randint(hot_key, (), 0, N_MEM)
        ranking = jax.random.permutation(order_key, pair_count)
        ranking = jnp.where(owner_of == hot_owner, ranking + pair_count, ranking)
        _, picked = lax.top_k(ranking, TOPK)
        local_pick = jax.vmap(unit_order)(jax.random.split(unit_key, N_MEM))
        units = owner_of * UNITS_DEV + local_pick[owner_of, slot_of]
        return units[picked].astype(jnp.int32)
    list_keys = jax.random.split(jax.random.fold_in(key, 17), NBLOCKS * KVH)
    return jax.vmap(one_list)(list_keys).reshape(NBLOCKS, KVH, TOPK)


def level_of(key, dims, pieces, least, high):
    gain = 1.0
    for dim, blocks in pieces:
        heights = jax.random.uniform(jax.random.fold_in(jax.random.fold_in(key, 6), dim), (blocks,), jnp.float32, least / len(pieces), high / len(pieces))
        gain = gain * jnp.repeat(jnp.exp(heights), dims[dim] // blocks).reshape((-1,) + (1,) * (len(dims) - 1 - dim))
    return gain


def bell_draw(own_key, shape, deviation, most, pieces=(), kind=jnp.bfloat16):
    drawn = jax.random.normal(own_key, shape, jnp.float32) * deviation
    if len(pieces) > 0:
        drawn = level_of(own_key, shape, pieces, -0.22, 0.18) * drawn
    return jnp.clip(drawn, min=-most, max=most).astype(kind)


def setup_inputs(seed: int = 0) -> dict:
    arg_keys = jax.random.split(jax.random.key(seed), 7)
    return {
        "query": draw_query(jax.random.fold_in(arg_keys[6], 71), 0),
        "new_keys": draw_new_keys(jax.random.fold_in(arg_keys[6], 71), 0),
        "new_values": bell_draw(arg_keys[2], (NBLOCKS, BLOCK_LEN, KVH, HD), 1.0, 5.0, ((0, 4), (1, 16), (2, 8))),
        "memory_keys": bell_draw(arg_keys[3], (UNITS, UNIT, KVH, HD), 1.0, 5.0, ((0, 16), (2, 8))),
        "memory_values": bell_draw(arg_keys[4], (UNITS, UNIT, KVH, HD), 1.0, 5.0, ((0, 16), (2, 8))),
        "retrieved": draw_retrieved(jax.random.fold_in(arg_keys[6], 71), 0),
    }


NEG = -1e+30

def reference(query, new_keys, new_values, memory_keys, memory_values, retrieved):
    score_scale = 1.0 / math.sqrt(HD)
    positions = jnp.arange(BLOCK_LEN, dtype=jnp.int32)
    causal = positions[None, :] <= positions[:, None]
    after = positions[None, :] > positions[:, None]

    def one_item(work_item):
        block_at = work_item // KVH
        head_at = work_item % KVH
        prior_at = jnp.maximum(block_at - 1, 0)
        queries = lax.dynamic_index_in_dim(lax.dynamic_index_in_dim(query, block_at, 0, False), head_at, 1, False)

        def pick(source, index_at):
            return lax.dynamic_index_in_dim(lax.dynamic_index_in_dim(source, index_at, 0, False), head_at, 1, False)
        unit_ids = lax.dynamic_index_in_dim(lax.dynamic_index_in_dim(retrieved, block_at, 0, False), head_at, 0, False)
        unit_keys = lax.dynamic_index_in_dim(memory_keys[unit_ids], head_at, 2, False).reshape(TOPK * UNIT, HD)
        unit_values = lax.dynamic_index_in_dim(memory_values[unit_ids], head_at, 2, False).reshape(TOPK * UNIT, HD)
        all_keys = jnp.concatenate([pick(new_keys, prior_at), pick(new_keys, block_at), unit_keys], axis=0)
        all_values = jnp.concatenate([pick(new_values, prior_at), pick(new_values, block_at), unit_values], axis=0)
        full_mask = jnp.concatenate([after & (block_at > 0), causal, jnp.ones((BLOCK_LEN, TOPK * UNIT), bool)], axis=1)
        scores = jnp.einsum('iqd,kd->iqk', queries.astype(jnp.float32), all_keys.astype(jnp.float32)) * score_scale
        scores = jnp.where(full_mask[:, None, :], scores, NEG)
        peak = lax.optimization_barrier(jnp.max(scores, axis=-1, keepdims=True))
        weights = jnp.where(full_mask[:, None, :], jnp.exp(scores - peak), 0.0)
        total = lax.optimization_barrier(jnp.sum(weights, axis=-1))
        rounded = lax.optimization_barrier(weights.astype(jnp.bfloat16)).astype(jnp.float32)
        summed = jnp.einsum('iqk,kd->iqd', rounded, all_values.astype(jnp.float32))
        return (summed / total[..., None]).astype(jnp.bfloat16)
    results = lax.map(one_item, jnp.arange(NBLOCKS * KVH, dtype=jnp.int32))
    results = results.reshape(NBLOCKS, KVH, BLOCK_LEN, QPK * HD)
    return jnp.transpose(results, (0, 2, 1, 3)).reshape(NBLOCKS, BLOCK_LEN, KVH * QPK * HD)
```

```python
import functools
import math

import jax
import jax.numpy as jnp
from jax import lax
from jax.experimental import pallas as pl
from jax.experimental.pallas import tpu as pltpu
from jax.sharding import PartitionSpec as P

MESH = pl.DeviceIdType.MESH
NEG = -1e30
LANES = 128
SLOTS = 3
ITEMS = 1 + SLOTS
ROWS = 256


def kernel(
    sizes,
    q_hbm,
    nk_hbm,
    nv_hbm,
    mk_hbm,
    mv_hbm,
    lists,
    o_ref,
    q_v,
    mk_v,
    mv_v,
    buf,
    prev,
    peak,
    accum,
    rows_f32,
    outgoing,
    local_sem,
    recv_sem,
    side_sem,
    up_sem,
    down_sem,
    prev_sem,
    out_send,
    out_recv,
):
    mem_count, head_count, span_count, unit_count, list_length, group, scale = sizes
    ring = mem_count // 2
    steps = ring // 2
    row_count = q_v.shape[0]
    block_rows = row_count // head_count
    mem = lax.axis_index("mem")
    head = lax.axis_index("head")
    span = lax.axis_index("span")
    z = mem // 2
    core = mem % 2

    def device(z_at, core_at, span_at, head_at=None):
        return {
            "mem": lax.rem(z_at + ring, ring) * 2 + core_at,
            "head": head if head_at is None else head_at,
            "span": lax.rem(span_at + span_count, span_count),
        }

    loads = [
        pltpu.make_async_copy(nk_hbm, buf.at[mem, 0, 0], local_sem.at[0]),
        pltpu.make_async_copy(nv_hbm, buf.at[mem, 1, 0], local_sem.at[1]),
        pltpu.make_async_copy(mk_hbm, mk_v, local_sem.at[2]),
        pltpu.make_async_copy(mv_hbm, mv_v, local_sem.at[3]),
        pltpu.make_async_copy(q_hbm, q_v, local_sem.at[4]),
    ]
    for load in loads:
        load.start()

    barrier = pltpu.get_barrier_semaphore()
    near = [
        (dz, 0, dx)
        for dz, dx in ((1, 0), (-1, 0), (0, 1), (0, -1), (1, 1), (-1, -1), (1, -1), (-1, 1))
    ]
    near += [(0, 1, 0), (0, 1, 1), (0, 1, -1)]
    for dz, dc, dx in near:
        pl.semaphore_signal(
            barrier,
            inc=1,
            device_id=device(z + dz, core if dc == 0 else 1 - core, span + dx),
            device_id_type=MESH,
        )
    for dy in range(1, head_count):
        pl.semaphore_signal(
            barrier,
            inc=1,
            device_id=device(z, core, span, lax.rem(head + dy, head_count)),
            device_id_type=MESH,
        )

    def owner(entry):
        return lists[0, entry] // unit_count

    loads[2].wait()
    loads[3].wait()
    picks = [jnp.int32(0)] * SLOTS
    rank = jnp.int32(0)
    for entry in range(list_length):
        here = owner(entry) == mem
        for slot in range(SLOTS):
            picks[slot] = jnp.where(
                here & (rank == slot), lists[0, entry] % unit_count, picks[slot]
            )
        rank = rank + here.astype(jnp.int32)
    for slot in range(SLOTS):
        buf[mem, 0, 1 + slot] = mk_v[picks[slot]]
        buf[mem, 1, 1 + slot] = mv_v[picks[slot]]
    loads[0].wait()
    loads[1].wait()
    loads[4].wait()
    pl.semaphore_wait(barrier, len(near) + head_count - 1)

    def transfer(source, item, send_sem, target):
        return pltpu.make_async_remote_copy(
            src_ref=buf.at[source, :, item],
            dst_ref=buf.at[source, :, item],
            send_sem=send_sem,
            recv_sem=recv_sem.at[source, item],
            device_id=target,
            device_id_type=MESH,
        )

    def send_up(source, item, step):
        shift = jnp.where((z == ring - 1) & (item == 0), 1, 0)
        return transfer(source, item, up_sem.at[step, item], device(z + 1, core, span + shift))

    def send_down(source, item, step):
        first = jnp.where(z > 0, 1, 0)
        later = jnp.where(z > 0, 0, -1)
        shift = jnp.where(item == 0, jnp.where(step == 0, first, later), 0)
        return transfer(source, item, down_sem.at[step, item], device(z - 1, core, span + shift))

    def send_side(source, item):
        own = source == mem
        shift = jnp.where(own & (item == 0), core, 0)
        return transfer(
            source, item, side_sem.at[source // 2, item], device(z, 1 - core, span + shift)
        )

    def send_prev():
        return pltpu.make_async_remote_copy(
            src_ref=buf.at[mem, :, 0],
            dst_ref=prev,
            send_sem=prev_sem.at[0],
            recv_sem=prev_sem.at[1],
            device_id=device(z, core, span + 1),
            device_id_type=MESH,
        )

    send_prev().start()
    for item in range(ITEMS):
        send_up(mem, item, 0).start()
        send_down(mem, item, 0).start()
        send_side(mem, item).start()

    def wait_item(source, item):
        send_side(source, item).wait_recv()

    def slot_bias(source):
        held = jnp.int32(0)
        for entry in range(list_length):
            held = held + (owner(entry) == source).astype(jnp.int32)
        return [
            jnp.full((1, LANES), jnp.where(held > slot, 0.0, NEG), jnp.float32)
            for slot in range(SLOTS)
        ]

    def block_bias(source):
        used = (source < mem) | (span > 0)
        return jnp.full((1, LANES), jnp.where(used, 0.0, NEG), jnp.float32)

    def source_bias(source):
        return jnp.concatenate([block_bias(source)] + slot_bias(source), axis=1)

    def keys_of(source):
        return buf[source, 0].reshape(ITEMS * LANES, LANES)

    def values_of(source):
        return buf[source, 1].reshape(ITEMS * LANES, LANES)

    def attend(start, count, keys, values, bias, fresh):
        rows = pl.ds(pl.multiple_of(start, count), count)
        width = keys.shape[0]
        scores = lax.dot_general(
            q_v[rows, :], keys, (((1,), (1,)), ((), ())), preferred_element_type=jnp.float32
        )
        scores = scores * scale + bias
        best = jnp.max(scores, axis=1, keepdims=True)
        if fresh:
            new_peak = jnp.broadcast_to(best, (count, LANES))
        else:
            old_peak = peak[rows, :]
            new_peak = jnp.maximum(old_peak, best)
        peak[rows, :] = new_peak
        weights = jnp.exp2(scores - jnp.concatenate([new_peak] * (width // LANES), axis=1))
        extended = jnp.concatenate([values, jnp.ones((width, LANES), jnp.bfloat16)], axis=1)
        update = jnp.dot(
            weights.astype(jnp.bfloat16), extended, preferred_element_type=jnp.float32
        )
        if fresh:
            result = update
        else:
            factor = jnp.exp2(old_peak - new_peak)
            result = accum[rows, :] * jnp.concatenate([factor, factor], axis=1) + update
        return rows, result

    send_prev().wait_recv()

    @pl.loop(0, row_count // ROWS)
    def _(block):
        start = block * ROWS
        position = (start + lax.broadcasted_iota(jnp.int32, (ROWS, LANES), 0)) // group
        column = lax.broadcasted_iota(jnp.int32, (ROWS, LANES), 1)
        causal = jnp.where(column <= position, 0.0, NEG)
        after = jnp.where((column > position) & (span > 0), 0.0, NEG)
        wide = [jnp.broadcast_to(b, (ROWS, LANES)) for b in slot_bias(mem)]
        bias = jnp.concatenate([causal] + wide + [after], axis=1)
        keys = jnp.concatenate([keys_of(mem), prev[0]], axis=0)
        values = jnp.concatenate([values_of(mem), prev[1]], axis=0)
        rows, result = attend(start, ROWS, keys, values, bias, True)
        accum[rows, :] = result

    def absorb(source):
        bias = source_bias(source)

        @pl.loop(0, row_count // ROWS)
        def _(block):
            rows, result = attend(
                block * ROWS, ROWS, keys_of(source), values_of(source), bias, False
            )
            accum[rows, :] = result

    def at(z_at, core_at):
        return lax.rem(z_at + ring, ring) * 2 + core_at

    @pl.loop(0, steps * ITEMS)
    def _(tick):
        step = tick // ITEMS + 1
        item = tick % ITEMS
        last = step == steps

        @pl.when(jnp.logical_not(last) | (item < ITEMS // 2))
        def _():
            below = at(z - step, core)
            wait_item(below, item)

            @pl.when((step < steps - 1) | ((step == steps - 1) & (item < ITEMS // 2)))
            def _():
                send_up(below, item, step).start()

            send_side(below, item).start()
            above = at(z + step, core)
            item_down = jnp.where(last, item + ITEMS // 2, item)
            wait_item(above, item_down)

            @pl.when((step < steps - 1) | ((step == steps - 1) & (item >= ITEMS // 2)))
            def _():
                send_down(above, item_down, step).start()

            send_side(above, item_down).start()

        @pl.when((step > 1) | (item == 0))
        def _():
            distance = jnp.where(item % 2 == 0, 1 - step, step - 1)
            other = (item >= ITEMS // 2) | (step == 1)
            source = at(z + distance, jnp.where(other, 1 - core, core))

            @pl.when(other)
            def _():
                for piece in range(ITEMS):
                    wait_item(source, piece)

            absorb(source)

    far = at(z + steps, core)
    far_side = at(z + steps, 1 - core)
    for piece in range(ITEMS):
        wait_item(far_side, piece)

    def send_out(target):
        return pltpu.make_async_remote_copy(
            src_ref=outgoing.at[target],
            dst_ref=o_ref.at[:, pl.ds(pl.multiple_of(head * group * LANES, LANES), group * LANES)],
            send_sem=out_send.at[target],
            recv_sem=out_recv.at[head],
            device_id=device(z, core, span, target),
            device_id_type=MESH,
        )

    def keep_out():
        return pltpu.make_async_copy(
            outgoing.at[head],
            o_ref.at[:, pl.ds(pl.multiple_of(head * group * LANES, LANES), group * LANES)],
            out_send.at[head],
        )

    far_bias = jnp.concatenate([source_bias(far), source_bias(far_side)], axis=1)

    @pl.loop(0, head_count)
    def _(turn):
        half = head_count // 2
        hop = jnp.where(turn % 2 == 0, half + turn // 2, half - (turn + 1) // 2)
        target = lax.rem(head + hop, head_count)
        keys = jnp.concatenate([keys_of(far), keys_of(far_side)], axis=0)
        values = jnp.concatenate([values_of(far), values_of(far_side)], axis=0)
        _, result = attend(target * block_rows, block_rows, keys, values, far_bias, False)
        rows_f32[...] = result[:, :LANES] / result[:, LANES:]
        for member in range(group):
            part = rows_f32[pl.ds(member, block_rows // group, stride=group), :]
            outgoing[target, :, member * LANES : (member + 1) * LANES] = part.astype(jnp.bfloat16)

        @pl.when(target != head)
        def _():
            send_out(target).start()

        @pl.when(target == head)
        def _():
            keep_out().start()

    send_prev().wait_send()

    @pl.loop(0, steps * ITEMS)
    def _(tick):
        step = tick // ITEMS
        item = tick % ITEMS

        @pl.when((step < steps - 1) | (item < ITEMS // 2))
        def _():
            send_up(at(z - step, core), item, step).wait_send()

        @pl.when((step < steps - 1) | (item >= ITEMS // 2))
        def _():
            send_down(at(z + step, core), item, step).wait_send()

    @pl.loop(0, ring * ITEMS)
    def _(tick):
        send_side(at(tick // ITEMS, core), tick % ITEMS).wait_send()

    keep_out().wait()

    @pl.loop(1, head_count)
    def _(hop):
        peer = lax.rem(head + hop, head_count)
        send_out(peer).wait_send()
        pltpu.make_async_remote_copy(
            src_ref=outgoing.at[peer],
            dst_ref=o_ref.at[:, pl.ds(pl.multiple_of(peer * group * LANES, LANES), group * LANES)],
            send_sem=out_send.at[peer],
            recv_sem=out_recv.at[peer],
            device_id=device(z, core, span, peer),
            device_id_type=MESH,
        ).wait_recv()


def local(query, new_keys, new_values, memory_keys, memory_values, retrieved):
    _, length, _, group, width = query.shape
    units, unit_length = memory_keys.shape[0], memory_keys.shape[1]
    mem_count = lax.axis_size("mem")
    head_count = lax.axis_size("head")
    span_count = lax.axis_size("span")
    list_length = retrieved.shape[2]
    ring = mem_count // 2
    steps = ring // 2
    rows = length * group
    scale = math.log2(math.e) / math.sqrt(width)
    sizes = (mem_count, head_count, span_count, units, list_length, group, scale)
    anywhere = pl.BlockSpec(memory_space=pl.ANY)
    dma = pltpu.SemaphoreType.DMA
    out = pl.pallas_call(
        functools.partial(kernel, sizes),
        out_shape=jax.ShapeDtypeStruct(
            (length // head_count, head_count * group * width), jnp.bfloat16
        ),
        in_specs=[anywhere] * 5 + [pl.BlockSpec(memory_space=pltpu.SMEM)],
        out_specs=anywhere,
        scratch_shapes=[
            pltpu.VMEM((rows, width), jnp.bfloat16),
            pltpu.VMEM((units, unit_length, width), jnp.bfloat16),
            pltpu.VMEM((units, unit_length, width), jnp.bfloat16),
            pltpu.VMEM((mem_count, 2, ITEMS, unit_length, width), jnp.bfloat16),
            pltpu.VMEM((2, length, width), jnp.bfloat16),
            pltpu.VMEM((rows, LANES), jnp.float32),
            pltpu.VMEM((rows, 2 * LANES), jnp.float32),
            pltpu.VMEM((rows // head_count, width), jnp.float32),
            pltpu.VMEM((head_count, length // head_count, group * width), jnp.bfloat16),
            dma((5,)),
            dma((mem_count, ITEMS)),
            dma((ring, ITEMS)),
            dma((steps, ITEMS)),
            dma((steps, ITEMS)),
            dma((2,)),
            dma((head_count,)),
            dma((head_count,)),
        ],
        compiler_params=pltpu.CompilerParams(
            collective_id=0, has_side_effects=True, vmem_limit_bytes=62 * 1024 * 1024
        ),
    )(
        query.reshape(rows, width),
        new_keys.reshape(length, width),
        new_values.reshape(length, width),
        memory_keys.reshape(units, unit_length, width),
        memory_values.reshape(units, unit_length, width),
        retrieved.reshape(1, list_length),
    )
    return out[None]


def solution(mesh):
    return jax.shard_map(
        local,
        mesh=mesh,
        in_specs=(
            P("span", "mem", "head", None, None),
            P("span", "mem", "head", None),
            P("span", "mem", "head", None),
            P("mem", None, "head", None),
            P("mem", None, "head", None),
            P("span", "head", None),
        ),
        out_specs=P("span", ("mem", "head"), None),
        check_vma=False,
    )
```

```python
import functools
import math

import jax
import jax.numpy as jnp
from jax import lax
from jax.experimental import pallas as pl
from jax.experimental.pallas import tpu as pltpu
from jax.sharding import PartitionSpec as P

MESH = pl.DeviceIdType.MESH
LANES = 128
SLOTS = 3
ITEMS = 1 + SLOTS
ROWS = 256
HUGE = 1e30


def kernel(
    sizes,
    q_hbm,
    nk_hbm,
    nv_hbm,
    mk_hbm,
    mv_hbm,
    lists,
    o_ref,
    q_v,
    mk_v,
    mv_v,
    buf,
    prev,
    peak,
    accum,
    rows_f32,
    outgoing,
    key_tiles,
    value_tiles,
    filler,
    local_sem,
    recv_sem,
    side_sem,
    up_sem,
    down_sem,
    prev_sem,
    out_send,
    out_recv,
):
    mem_count, head_count, span_count, unit_count, list_length, group, scale = sizes
    ring = mem_count // 2
    steps = ring // 2
    row_count = q_v.shape[0]
    block_rows = row_count // head_count
    mem = lax.axis_index("mem")
    head = lax.axis_index("head")
    span = lax.axis_index("span")
    z = mem // 2
    core = mem % 2

    def device(z_at, core_at, span_at, head_at=None):
        return {
            "mem": lax.rem(z_at + ring, ring) * 2 + core_at,
            "head": head if head_at is None else head_at,
            "span": lax.rem(span_at + span_count, span_count),
        }

    loads = [
        pltpu.make_async_copy(nk_hbm, buf.at[mem, 0, 0], local_sem.at[0]),
        pltpu.make_async_copy(nv_hbm, buf.at[mem, 1, 0], local_sem.at[1]),
        pltpu.make_async_copy(mk_hbm, mk_v, local_sem.at[2]),
        pltpu.make_async_copy(mv_hbm, mv_v, local_sem.at[3]),
        pltpu.make_async_copy(q_hbm, q_v, local_sem.at[4]),
    ]
    for load in loads:
        load.start()

    barrier = pltpu.get_barrier_semaphore()
    near = [
        (dz, 0, dx)
        for dz, dx in ((1, 0), (-1, 0), (0, 1), (0, -1), (1, 1), (-1, -1), (1, -1), (-1, 1))
    ]
    near += [(0, 1, 0), (0, 1, 1), (0, 1, -1)]
    for dz, dc, dx in near:
        pl.semaphore_signal(
            barrier,
            inc=1,
            device_id=device(z + dz, core if dc == 0 else 1 - core, span + dx),
            device_id_type=MESH,
        )
    for dy in range(1, head_count):
        pl.semaphore_signal(
            barrier,
            inc=1,
            device_id=device(z, core, span, lax.rem(head + dy, head_count)),
            device_id_type=MESH,
        )

    def owner(entry):
        return lists[0, entry] // unit_count

    loads[2].wait()
    loads[3].wait()
    picks = [jnp.int32(0)] * SLOTS
    rank = jnp.int32(0)
    for entry in range(list_length):
        here = owner(entry) == mem
        for slot in range(SLOTS):
            picks[slot] = jnp.where(
                here & (rank == slot), lists[0, entry] % unit_count, picks[slot]
            )
        rank = rank + here.astype(jnp.int32)
    for slot in range(SLOTS):
        buf[mem, 0, 1 + slot] = mk_v[picks[slot]]
        buf[mem, 1, 1 + slot] = mv_v[picks[slot]]
    loads[0].wait()
    loads[1].wait()
    loads[4].wait()
    pl.semaphore_wait(barrier, len(near) + head_count - 1)

    def transfer(source, item, send_sem, target):
        return pltpu.make_async_remote_copy(
            src_ref=buf.at[source, :, item],
            dst_ref=buf.at[source, :, item],
            send_sem=send_sem,
            recv_sem=recv_sem.at[source, item],
            device_id=target,
            device_id_type=MESH,
        )

    def send_up(source, item, step):
        shift = jnp.where((z == ring - 1) & (item == 0), 1, 0)
        return transfer(source, item, up_sem.at[step, item], device(z + 1, core, span + shift))

    def send_down(source, item, step):
        first = jnp.where(z > 0, 1, 0)
        later = jnp.where(z > 0, 0, -1)
        shift = jnp.where(item == 0, jnp.where(step == 0, first, later), 0)
        return transfer(source, item, down_sem.at[step, item], device(z - 1, core, span + shift))

    def send_side(source, item):
        own = source == mem
        shift = jnp.where(own & (item == 0), core, 0)
        return transfer(
            source, item, side_sem.at[source // 2, item], device(z, 1 - core, span + shift)
        )

    def send_prev():
        return pltpu.make_async_remote_copy(
            src_ref=buf.at[mem, :, 0],
            dst_ref=prev,
            send_sem=prev_sem.at[0],
            recv_sem=prev_sem.at[1],
            device_id=device(z, core, span + 1),
            device_id_type=MESH,
        )

    send_prev().start()
    for item in range(ITEMS):
        send_up(mem, item, 0).start()
        send_down(mem, item, 0).start()
        send_side(mem, item).start()

    def wait_item(source, item):
        send_side(source, item).wait_recv()

    filler[...] = jnp.broadcast_to(buf[mem, 0, 0, 0:1, :], filler.shape)

    def flags_of(source):
        held = jnp.int32(0)
        for entry in range(list_length):
            held = held + (owner(entry) == source).astype(jnp.int32)
        used = (source < mem) | (span > 0) | (source == mem)
        return [used] + [held > slot for slot in range(SLOTS)]

    def stage(source, base):
        for item, flag in enumerate(flags_of(source)):
            tile = pl.ds((base + item) * LANES, LANES)
            key_tiles[tile, :] = jnp.where(flag, buf[source, 0, item], filler[...])
            value_tiles[tile, :LANES] = jnp.where(flag, buf[source, 1, item], jnp.bfloat16(0))
            value_tiles[tile, LANES:] = jnp.full(
                (LANES, LANES), jnp.where(flag, 1.0, 0.0), jnp.float32
            ).astype(jnp.bfloat16)

    def score(rows, width, masks):
        scores = lax.dot_general(
            q_v[rows, :],
            key_tiles[:width, :],
            (((1,), (1,)), ((), ())),
            preferred_element_type=jnp.float32,
        )
        if masks:
            tiles = [scores[:, t * LANES : (t + 1) * LANES] for t in range(width // LANES)]
            for t, mask in masks.items():
                tiles[t] = jnp.where(mask, tiles[t], -HUGE)
            scores = jnp.concatenate(tiles, axis=1)
        return scores

    def weigh(rows, width, scores, fresh):
        best = jnp.max(scores, axis=1, keepdims=True)
        factor = None
        if fresh:
            new_peak = jnp.broadcast_to(best, (scores.shape[0], LANES))
        else:
            old_peak = peak[rows, :]
            new_peak = jnp.maximum(old_peak, best)
            factor = jnp.exp2((old_peak - new_peak) * scale)
        wide_peak = jnp.concatenate([new_peak] * (width // LANES), axis=1)
        weights = jnp.exp2((scores - wide_peak) * scale)
        return new_peak, factor, weights.astype(jnp.bfloat16)

    def combine(rows, width, weights, factor):
        result = jnp.dot(weights, value_tiles[:width, :], preferred_element_type=jnp.float32)
        if factor is not None:
            result = accum[rows, :] * jnp.concatenate([factor, factor], axis=1) + result
        return result

    def attend_all(blocks, width, masks_of, fresh, finish):
        count = len(blocks)
        scores = score(blocks[0], width, masks_of(0))
        weighed = None
        for index in range(count + 1):
            following = None
            if index + 1 < count:
                following = score(blocks[index + 1], width, masks_of(index + 1))
            done = weighed
            if index < count:
                weighed = weigh(blocks[index], width, scores, fresh)
            if done is not None:
                new_peak, factor, weights = done
                finish(index - 1, new_peak, combine(blocks[index - 1], width, weights, factor))
            scores = following

    send_prev().wait_recv()
    stage(mem, 0)
    own_tile = pl.ds(ITEMS * LANES, LANES)
    key_tiles[own_tile, :] = prev[0]
    value_tiles[own_tile, :LANES] = prev[1]
    value_tiles[own_tile, LANES:] = jnp.ones((LANES, LANES), jnp.bfloat16)
    blocks = [pl.ds(start, ROWS) for start in range(0, row_count, ROWS)]

    def own_masks(index):
        position = (index * ROWS + lax.broadcasted_iota(jnp.int32, (ROWS, LANES), 0)) // group
        column = lax.broadcasted_iota(jnp.int32, (ROWS, LANES), 1)
        return {0: column <= position, ITEMS: (column > position) & (span > 0)}

    def keep(index, new_peak, result):
        peak[blocks[index], :] = new_peak
        accum[blocks[index], :] = result

    attend_all(blocks, (ITEMS + 1) * LANES, own_masks, True, keep)

    def absorb(source):
        stage(source, 0)
        attend_all(blocks, ITEMS * LANES, lambda index: {}, False, keep)

    def at(z_at, core_at):
        return lax.rem(z_at + ring, ring) * 2 + core_at

    @pl.loop(0, steps * ITEMS)
    def _(tick):
        step = tick // ITEMS + 1
        item = tick % ITEMS
        last = step == steps

        @pl.when(jnp.logical_not(last) | (item < ITEMS // 2))
        def _():
            below = at(z - step, core)
            wait_item(below, item)

            @pl.when((step < steps - 1) | ((step == steps - 1) & (item < ITEMS // 2)))
            def _():
                send_up(below, item, step).start()

            send_side(below, item).start()
            above = at(z + step, core)
            item_down = jnp.where(last, item + ITEMS // 2, item)
            wait_item(above, item_down)

            @pl.when((step < steps - 1) | ((step == steps - 1) & (item >= ITEMS // 2)))
            def _():
                send_down(above, item_down, step).start()

            send_side(above, item_down).start()

        @pl.when((step > 1) | (item == 0))
        def _():
            distance = jnp.where(item % 2 == 0, 1 - step, step - 1)
            other = (item >= ITEMS // 2) | (step == 1)
            source = at(z + distance, jnp.where(other, 1 - core, core))

            @pl.when(other)
            def _():
                for piece in range(ITEMS):
                    wait_item(source, piece)

            absorb(source)

    far = at(z + steps, core)
    far_side = at(z + steps, 1 - core)
    for piece in range(ITEMS):
        wait_item(far_side, piece)

    def send_out(target):
        return pltpu.make_async_remote_copy(
            src_ref=outgoing.at[target],
            dst_ref=o_ref.at[:, pl.ds(pl.multiple_of(head * group * LANES, LANES), group * LANES)],
            send_sem=out_send.at[target],
            recv_sem=out_recv.at[head],
            device_id=device(z, core, span, target),
            device_id_type=MESH,
        )

    def keep_out():
        return pltpu.make_async_copy(
            outgoing.at[head],
            o_ref.at[:, pl.ds(pl.multiple_of(head * group * LANES, LANES), group * LANES)],
            out_send.at[head],
        )

    stage(far, 0)
    stage(far_side, ITEMS)
    half = head_count // 2
    hops = [half]
    for hop in range(1, half):
        hops += [half - hop, half + hop]
    hops += [0]
    targets = [lax.rem(head + hop, head_count) for hop in hops]
    parts = [
        pl.ds(pl.multiple_of(target * block_rows, block_rows), block_rows) for target in targets
    ]

    def hand_over(turn, new_peak, result):
        target = targets[turn]
        rows_f32[turn % 2] = result[:, :LANES] / result[:, LANES:]
        for member in range(group):
            part = rows_f32[turn % 2, pl.ds(member, block_rows // group, stride=group), :]
            outgoing[target, :, member * LANES : (member + 1) * LANES] = part.astype(jnp.bfloat16)
        if hops[turn] > 0:
            send_out(target).start()
        else:
            keep_out().start()

    attend_all(parts, 2 * ITEMS * LANES, lambda turn: {}, False, hand_over)

    send_prev().wait_send()

    @pl.loop(0, steps * ITEMS)
    def _(tick):
        step = tick // ITEMS
        item = tick % ITEMS

        @pl.when((step < steps - 1) | (item < ITEMS // 2))
        def _():
            send_up(at(z - step, core), item, step).wait_send()

        @pl.when((step < steps - 1) | (item >= ITEMS // 2))
        def _():
            send_down(at(z + step, core), item, step).wait_send()

    @pl.loop(0, ring * ITEMS)
    def _(tick):
        send_side(at(tick // ITEMS, core), tick % ITEMS).wait_send()

    keep_out().wait()

    @pl.loop(1, head_count)
    def _(hop):
        peer = lax.rem(head + hop, head_count)
        send_out(peer).wait_send()
        pltpu.make_async_remote_copy(
            src_ref=outgoing.at[peer],
            dst_ref=o_ref.at[:, pl.ds(pl.multiple_of(peer * group * LANES, LANES), group * LANES)],
            send_sem=out_send.at[peer],
            recv_sem=out_recv.at[peer],
            device_id=device(z, core, span, peer),
            device_id_type=MESH,
        ).wait_recv()


def local(query, new_keys, new_values, memory_keys, memory_values, retrieved):
    _, length, _, group, width = query.shape
    units, unit_length = memory_keys.shape[0], memory_keys.shape[1]
    mem_count = lax.axis_size("mem")
    head_count = lax.axis_size("head")
    span_count = lax.axis_size("span")
    list_length = retrieved.shape[2]
    ring = mem_count // 2
    steps = ring // 2
    rows = length * group
    scale = math.log2(math.e) / math.sqrt(width)
    sizes = (mem_count, head_count, span_count, units, list_length, group, scale)
    anywhere = pl.BlockSpec(memory_space=pl.ANY)
    dma = pltpu.SemaphoreType.DMA
    out = pl.pallas_call(
        functools.partial(kernel, sizes),
        out_shape=jax.ShapeDtypeStruct(
            (length // head_count, head_count * group * width), jnp.bfloat16
        ),
        in_specs=[anywhere] * 5 + [pl.BlockSpec(memory_space=pltpu.SMEM)],
        out_specs=anywhere,
        scratch_shapes=[
            pltpu.VMEM((rows, width), jnp.bfloat16),
            pltpu.VMEM((units, unit_length, width), jnp.bfloat16),
            pltpu.VMEM((units, unit_length, width), jnp.bfloat16),
            pltpu.VMEM((mem_count, 2, ITEMS, unit_length, width), jnp.bfloat16),
            pltpu.VMEM((2, length, width), jnp.bfloat16),
            pltpu.VMEM((rows, LANES), jnp.float32),
            pltpu.VMEM((rows, 2 * LANES), jnp.float32),
            pltpu.VMEM((2, rows // head_count, width), jnp.float32),
            pltpu.VMEM((head_count, length // head_count, group * width), jnp.bfloat16),
            pltpu.VMEM((2 * ITEMS * unit_length, width), jnp.bfloat16),
            pltpu.VMEM((2 * ITEMS * unit_length, 2 * width), jnp.bfloat16),
            pltpu.VMEM((unit_length, width), jnp.bfloat16),
            dma((5,)),
            dma((mem_count, ITEMS)),
            dma((ring, ITEMS)),
            dma((steps, ITEMS)),
            dma((steps, ITEMS)),
            dma((2,)),
            dma((head_count,)),
            dma((head_count,)),
        ],
        compiler_params=pltpu.CompilerParams(
            collective_id=0, has_side_effects=True, vmem_limit_bytes=62 * 1024 * 1024
        ),
    )(
        query.reshape(rows, width),
        new_keys.reshape(length, width),
        new_values.reshape(length, width),
        memory_keys.reshape(units, unit_length, width),
        memory_values.reshape(units, unit_length, width),
        retrieved.reshape(1, list_length),
    )
    return out[None]


def solution(mesh):
    return jax.shard_map(
        local,
        mesh=mesh,
        in_specs=(
            P("span", "mem", "head", None, None),
            P("span", "mem", "head", None),
            P("span", "mem", "head", None),
            P("mem", None, "head", None),
            P("mem", None, "head", None),
            P("span", "head", None),
        ),
        out_specs=P("span", ("mem", "head"), None),
        check_vma=False,
    )
```

```python
import functools
import math

import jax
import jax.numpy as jnp
from jax import lax
from jax.experimental import pallas as pl
from jax.experimental.pallas import tpu as pltpu
from jax.sharding import PartitionSpec as P

MESH = pl.DeviceIdType.MESH
LANES = 128
SLOTS = 3
ITEMS = 1 + SLOTS
ROWS = 256
HUGE = 1e30


def kernel(
    sizes,
    q_hbm,
    nk_hbm,
    nv_hbm,
    mk_hbm,
    mv_hbm,
    lists,
    o_ref,
    q_v,
    mk_v,
    mv_v,
    buf,
    far,
    prev,
    peak,
    accum,
    rows_f32,
    outgoing,
    key_tiles,
    value_tiles,
    filler,
    table,
    local_sem,
    recv_sem,
    far_sem,
    side_sem,
    far_side_sem,
    up_sem,
    down_sem,
    prev_sem,
    out_send,
    out_recv,
):
    mem_count, head_count, span_count, unit_count, list_length, group, scale = sizes
    ring = mem_count // 2
    steps = ring // 2
    row_count = q_v.shape[0]
    block_rows = row_count // head_count
    mem = lax.axis_index("mem")
    head = lax.axis_index("head")
    span = lax.axis_index("span")
    z = mem // 2
    core = mem % 2

    def device(z_at, core_at, span_at, head_at=None):
        return {
            "mem": lax.rem(z_at + ring, ring) * 2 + core_at,
            "head": head if head_at is None else head_at,
            "span": lax.rem(span_at + span_count, span_count),
        }

    loads = [
        pltpu.make_async_copy(nk_hbm, buf.at[mem, 0, 0], local_sem.at[0]),
        pltpu.make_async_copy(nv_hbm, buf.at[mem, 1, 0], local_sem.at[1]),
        pltpu.make_async_copy(mk_hbm, mk_v, local_sem.at[2]),
        pltpu.make_async_copy(mv_hbm, mv_v, local_sem.at[3]),
        pltpu.make_async_copy(q_hbm, q_v, local_sem.at[4]),
    ]
    for load in loads:
        load.start()

    barrier = pltpu.get_barrier_semaphore()
    near = [
        (dz, 0, dx)
        for dz, dx in ((1, 0), (-1, 0), (0, 1), (0, -1), (1, 1), (-1, -1), (1, -1), (-1, 1))
    ]
    near += [(0, 1, 0), (0, 1, 1), (0, 1, -1)]
    for dz, dc, dx in near:
        pl.semaphore_signal(
            barrier,
            inc=1,
            device_id=device(z + dz, core if dc == 0 else 1 - core, span + dx),
            device_id_type=MESH,
        )
    for dy in range(1, head_count):
        pl.semaphore_signal(
            barrier,
            inc=1,
            device_id=device(z, core, span, lax.rem(head + dy, head_count)),
            device_id_type=MESH,
        )

    def owner(entry):
        return lists[0, entry] // unit_count

    def at(z_at, core_at):
        return lax.rem(z_at + ring, ring) * 2 + core_at

    far_z = lax.rem(z + steps, ring)

    def transfer(source, item, send_sem, target, last=False):
        if last:
            landing, landed = far.at[core, :, item], far_sem.at[core, item]
        else:
            landing, landed = buf.at[source, :, item], recv_sem.at[source, item]
        return pltpu.make_async_remote_copy(
            src_ref=buf.at[source, :, item],
            dst_ref=landing,
            send_sem=send_sem,
            recv_sem=landed,
            device_id=target,
            device_id_type=MESH,
        )

    def send_up(source, item, step, last=False):
        shift = jnp.where((z == ring - 1) & (item == 0), 1, 0)
        target = device(z + 1, core, span + shift)
        return transfer(source, item, up_sem.at[step, item], target, last)

    def send_down(source, item, step, last=False):
        first = jnp.where(z > 0, 1, 0)
        later = jnp.where(z > 0, 0, -1)
        shift = jnp.where(item == 0, jnp.where(step == 0, first, later), 0)
        target = device(z - 1, core, span + shift)
        return transfer(source, item, down_sem.at[step, item], target, last)

    def send_side(source, item):
        own = source == mem
        shift = jnp.where(own & (item == 0), core, 0)
        return transfer(
            source, item, side_sem.at[source // 2, item], device(z, 1 - core, span + shift)
        )

    def far_copy(origin, item):
        return pltpu.make_async_remote_copy(
            src_ref=far.at[origin, :, item],
            dst_ref=far.at[origin, :, item],
            send_sem=far_side_sem.at[item],
            recv_sem=far_sem.at[origin, item],
            device_id=device(z, 1 - core, span),
            device_id_type=MESH,
        )

    def send_prev():
        return pltpu.make_async_remote_copy(
            src_ref=buf.at[mem, :, 0],
            dst_ref=prev,
            send_sem=prev_sem.at[0],
            recv_sem=prev_sem.at[1],
            device_id=device(z, core, span + 1),
            device_id_type=MESH,
        )

    def wait_item(source, item):
        send_side(source, item).wait_recv()

    def send_own(item):
        send_up(mem, item, 0).start()
        send_down(mem, item, 0).start()
        send_side(mem, item).start()

    loads[0].wait()
    loads[1].wait()
    pl.semaphore_wait(barrier, len(near) + head_count - 1)
    send_own(0)
    send_prev().start()

    owners = [owner(entry) for entry in range(list_length)]
    picks = [jnp.int32(0)] * SLOTS
    rank = jnp.int32(0)
    for entry in range(list_length):
        here = owners[entry] == mem
        for slot in range(SLOTS):
            picks[slot] = jnp.where(
                here & (rank == slot), lists[0, entry] % unit_count, picks[slot]
            )
        rank = rank + here.astype(jnp.int32)
    loads[2].wait()
    loads[3].wait()
    for slot in range(SLOTS):
        buf[mem, 0, 1 + slot] = mk_v[picks[slot]]
        buf[mem, 1, 1 + slot] = mv_v[picks[slot]]
    filler[...] = jnp.broadcast_to(buf[mem, 0, 0, 0:1, :], filler.shape)

    ranks = []
    for entry in range(list_length):
        same = jnp.int32(0)
        for earlier in range(entry):
            same = same + (owners[earlier] == owners[entry]).astype(jnp.int32)
        ranks.append(same)
    for item in range(1, ITEMS):
        send_own(item)
    distant = [(held // 2 == far_z).astype(jnp.int32) for held in owners]
    place_far = jnp.int32(list_length) - sum(distant)
    place_near = jnp.int32(0)
    places = []
    for entry in range(list_length):
        places.append(jnp.where(distant[entry] == 1, place_far, place_near))
        place_far = place_far + distant[entry]
        place_near = place_near + 1 - distant[entry]
    for place in range(list_length):
        code = jnp.int32(0)
        for entry in range(list_length):
            value = owners[entry] * ITEMS + 1 + ranks[entry]
            code = code + jnp.where(places[entry] == place, value, 0)
        table[place] = code
    loads[4].wait()

    def put(tile, keys, values, ones):
        tile = pl.ds(tile * LANES, LANES)
        key_tiles[tile, :] = keys
        value_tiles[tile, :LANES] = values
        value_tiles[tile, LANES:] = ones

    ones = jnp.ones((LANES, LANES), jnp.bfloat16)

    def put_chunk(tile, source, keys, values):
        used = (source < mem) | (span > 0)
        weight = jnp.full((LANES, LANES), jnp.where(used, 1.0, 0.0), jnp.float32)
        put(
            tile,
            jnp.where(used, keys, filler[...]),
            jnp.where(used, values, jnp.bfloat16(0)),
            weight.astype(jnp.bfloat16),
        )

    def put_unit(tile, place, maybe_far):
        held = table[place] // ITEMS
        item = table[place] % ITEMS
        pair = [buf[held, kind, item] for kind in range(2)]
        if maybe_far:
            there = held // 2 == far_z
            pair = [
                jnp.where(there, far[held % 2, kind, item], pair[kind]) for kind in range(2)
            ]
        put(tile, pair[0], pair[1], ones)

    def score(rows, width, masks):
        scores = lax.dot_general(
            q_v[rows, :],
            key_tiles[:width, :],
            (((1,), (1,)), ((), ())),
            preferred_element_type=jnp.float32,
        )
        if masks:
            tiles = [scores[:, t * LANES : (t + 1) * LANES] for t in range(width // LANES)]
            for t, mask in masks.items():
                tiles[t] = jnp.where(mask, tiles[t], -HUGE)
            scores = jnp.concatenate(tiles, axis=1)
        return scores

    def weigh(rows, width, scores, fresh):
        best = jnp.max(scores, axis=1, keepdims=True)
        factor = None
        if fresh:
            new_peak = jnp.broadcast_to(best, (scores.shape[0], LANES))
        else:
            old_peak = peak[rows, :]
            new_peak = jnp.maximum(old_peak, best)
            factor = jnp.exp2((old_peak - new_peak) * scale)
        wide_peak = jnp.concatenate([new_peak] * (width // LANES), axis=1)
        weights = jnp.exp2((scores - wide_peak) * scale)
        return new_peak, factor, weights.astype(jnp.bfloat16)

    def combine(rows, width, weights, factor):
        result = jnp.dot(weights, value_tiles[:width, :], preferred_element_type=jnp.float32)
        if factor is not None:
            result = accum[rows, :] * jnp.concatenate([factor, factor], axis=1) + result
        return result

    def attend_all(blocks, width, masks_of, fresh, finish):
        count = len(blocks)
        scores = score(blocks[0], width, masks_of(0))
        weighed = None
        for index in range(count + 1):
            following = None
            if index + 1 < count:
                following = score(blocks[index + 1], width, masks_of(index + 1))
            done = weighed
            if index < count:
                weighed = weigh(blocks[index], width, scores, fresh)
            if done is not None:
                new_peak, factor, weights = done
                finish(index - 1, new_peak, combine(blocks[index - 1], width, weights, factor))
            scores = following

    put(0, buf[mem, 0, 0], buf[mem, 1, 0], ones)
    beside = at(z, 1 - core)
    wait_item(beside, 0)
    put_chunk(1, beside, buf[beside, 0, 0], buf[beside, 1, 0])
    send_prev().wait_recv()
    put(2, prev[0], prev[1], ones)
    blocks = [pl.ds(start, ROWS) for start in range(0, row_count, ROWS)]

    def own_masks(index):
        position = (index * ROWS + lax.broadcasted_iota(jnp.int32, (ROWS, LANES), 0)) // group
        column = lax.broadcasted_iota(jnp.int32, (ROWS, LANES), 1)
        return {0: column <= position, 2: (column > position) & (span > 0)}

    def keep(index, new_peak, result):
        peak[blocks[index], :] = new_peak
        accum[blocks[index], :] = result

    attend_all(blocks, 3 * LANES, own_masks, True, keep)

    def absorb(tiles):
        attend_all(blocks, tiles * LANES, lambda index: {}, False, keep)

    @pl.loop(0, (steps - 1) * ITEMS)
    def _(tick):
        step = tick // ITEMS + 1
        item = tick % ITEMS
        turning = step == steps - 1
        below = at(z - step, core)
        wait_item(below, item)

        @pl.when(jnp.logical_not(turning))
        def _():
            send_up(below, item, step).start()

        @pl.when(turning & (item < ITEMS // 2))
        def _():
            send_up(below, item, step, True).start()

        send_side(below, item).start()
        above = at(z + step, core)
        wait_item(above, item)

        @pl.when(jnp.logical_not(turning))
        def _():
            send_down(above, item, step).start()

        @pl.when(turning & (item >= ITEMS // 2))
        def _():
            send_down(above, item, step, True).start()

        send_side(above, item).start()

        @pl.when(item == 1)
        def _():
            for tile, (distance, core_at) in enumerate(
                ((-step, core), (step, core), (-step, 1 - core), (step, 1 - core))
            ):
                source = at(z + distance, core_at)
                if tile >= 2:
                    wait_item(source, 0)
                put_chunk(tile, source, buf[source, 0, 0], buf[source, 1, 0])
            absorb(4)

    early = min(list_length // 2, list_length - 2 * SLOTS)
    for item in range(1, ITEMS):
        wait_item(beside, item)

    @pl.loop(0, (steps - 1) * (ITEMS - 1))
    def _(tick):
        step = tick // (ITEMS - 1) + 1
        item = tick % (ITEMS - 1) + 1
        wait_item(at(z - step, 1 - core), item)
        wait_item(at(z + step, 1 - core), item)

    for half in range(2):
        for item in (half, half + ITEMS // 2):
            far_copy(core, item).wait_recv()
            far_copy(core, item).start()
        first, past = half * early // 2, (half + 1) * early // 2
        for place in range(first, past):
            put_unit(place - first, place, False)
        absorb(past - first)

    for item in range(ITEMS):
        far_copy(1 - core, item).wait_recv()

    def send_out(target):
        return pltpu.make_async_remote_copy(
            src_ref=outgoing.at[target],
            dst_ref=o_ref.at[:, pl.ds(pl.multiple_of(head * group * LANES, LANES), group * LANES)],
            send_sem=out_send.at[target],
            recv_sem=out_recv.at[head],
            device_id=device(z, core, span, target),
            device_id_type=MESH,
        )

    def keep_out():
        return pltpu.make_async_copy(
            outgoing.at[head],
            o_ref.at[:, pl.ds(pl.multiple_of(head * group * LANES, LANES), group * LANES)],
            out_send.at[head],
        )

    for origin in range(2):
        put_chunk(origin, far_z * 2 + origin, far[origin, 0, 0], far[origin, 1, 0])
    for place in range(early, list_length):
        put_unit(2 + place - early, place, True)
    half = head_count // 2
    hops = [half]
    for hop in range(1, half):
        hops += [half - hop, half + hop]
    hops += [0]
    targets = [lax.rem(head + hop, head_count) for hop in hops]
    parts = [
        pl.ds(pl.multiple_of(target * block_rows, block_rows), block_rows) for target in targets
    ]

    def hand_over(turn, new_peak, result):
        target = targets[turn]
        rows_f32[turn % 2] = result[:, :LANES] / result[:, LANES:]
        for member in range(group):
            part = rows_f32[turn % 2, pl.ds(member, block_rows // group, stride=group), :]
            outgoing[target, :, member * LANES : (member + 1) * LANES] = part.astype(jnp.bfloat16)
        if hops[turn] > 0:
            send_out(target).start()
        else:
            keep_out().start()

    attend_all(parts, (2 + list_length - early) * LANES, lambda turn: {}, False, hand_over)

    send_prev().wait_send()

    @pl.loop(0, (steps - 1) * ITEMS)
    def _(tick):
        step = tick // ITEMS
        item = tick % ITEMS
        send_up(at(z - step, core), item, step).wait_send()
        send_down(at(z + step, core), item, step).wait_send()
        send_side(at(z - step, core), item).wait_send()

        @pl.when(step > 0)
        def _():
            send_side(at(z + step, core), item).wait_send()

    for item in range(ITEMS // 2):
        send_up(at(z - steps + 1, core), item, steps - 1, True).wait_send()
        send_down(at(z + steps - 1, core), item + ITEMS // 2, steps - 1, True).wait_send()

    @pl.loop(0, ITEMS)
    def _(item):
        for step in (1 - steps, steps - 1):
            send_side(at(z + step, core), item).wait_send()
        far_copy(core, item).wait_send()

    keep_out().wait()

    @pl.loop(1, head_count)
    def _(hop):
        peer = lax.rem(head + hop, head_count)
        send_out(peer).wait_send()
        pltpu.make_async_remote_copy(
            src_ref=outgoing.at[peer],
            dst_ref=o_ref.at[:, pl.ds(pl.multiple_of(peer * group * LANES, LANES), group * LANES)],
            send_sem=out_send.at[peer],
            recv_sem=out_recv.at[peer],
            device_id=device(z, core, span, peer),
            device_id_type=MESH,
        ).wait_recv()


def local(query, new_keys, new_values, memory_keys, memory_values, retrieved):
    _, length, _, group, width = query.shape
    units, unit_length = memory_keys.shape[0], memory_keys.shape[1]
    mem_count = lax.axis_size("mem")
    head_count = lax.axis_size("head")
    span_count = lax.axis_size("span")
    list_length = retrieved.shape[2]
    ring = mem_count // 2
    steps = ring // 2
    rows = length * group
    tiles = 2 + max(list_length, 2 * SLOTS)
    scale = math.log2(math.e) / math.sqrt(width)
    sizes = (mem_count, head_count, span_count, units, list_length, group, scale)
    anywhere = pl.BlockSpec(memory_space=pl.ANY)
    dma = pltpu.SemaphoreType.DMA
    out = pl.pallas_call(
        functools.partial(kernel, sizes),
        out_shape=jax.ShapeDtypeStruct(
            (length // head_count, head_count * group * width), jnp.bfloat16
        ),
        in_specs=[anywhere] * 5 + [pl.BlockSpec(memory_space=pltpu.SMEM)],
        out_specs=anywhere,
        scratch_shapes=[
            pltpu.VMEM((rows, width), jnp.bfloat16),
            pltpu.VMEM((units, unit_length, width), jnp.bfloat16),
            pltpu.VMEM((units, unit_length, width), jnp.bfloat16),
            pltpu.VMEM((mem_count, 2, ITEMS, unit_length, width), jnp.bfloat16),
            pltpu.VMEM((2, 2, ITEMS, unit_length, width), jnp.bfloat16),
            pltpu.VMEM((2, length, width), jnp.bfloat16),
            pltpu.VMEM((rows, LANES), jnp.float32),
            pltpu.VMEM((rows, 2 * LANES), jnp.float32),
            pltpu.VMEM((2, rows // head_count, width), jnp.float32),
            pltpu.VMEM((head_count, length // head_count, group * width), jnp.bfloat16),
            pltpu.VMEM((tiles * unit_length, width), jnp.bfloat16),
            pltpu.VMEM((tiles * unit_length, 2 * width), jnp.bfloat16),
            pltpu.VMEM((unit_length, width), jnp.bfloat16),
            pltpu.SMEM((list_length,), jnp.int32),
            dma((5,)),
            dma((mem_count, ITEMS)),
            dma((2, ITEMS)),
            dma((ring, ITEMS)),
            dma((ITEMS,)),
            dma((steps, ITEMS)),
            dma((steps, ITEMS)),
            dma((2,)),
            dma((head_count,)),
            dma((head_count,)),
        ],
        compiler_params=pltpu.CompilerParams(
            collective_id=0, has_side_effects=True, vmem_limit_bytes=62 * 1024 * 1024
        ),
    )(
        query.reshape(rows, width),
        new_keys.reshape(length, width),
        new_values.reshape(length, width),
        memory_keys.reshape(units, unit_length, width),
        memory_values.reshape(units, unit_length, width),
        retrieved.reshape(1, list_length),
    )
    return out[None]


def solution(mesh):
    return jax.shard_map(
        local,
        mesh=mesh,
        in_specs=(
            P("span", "mem", "head", None, None),
            P("span", "mem", "head", None),
            P("span", "mem", "head", None),
            P("mem", None, "head", None),
            P("mem", None, "head", None),
            P("span", "head", None),
        ),
        out_specs=P("span", ("mem", "head"), None),
        check_vma=False,
    )
```

```python
import functools
import math

import jax
import jax.numpy as jnp
from jax import lax
from jax.experimental import pallas as pl
from jax.experimental.pallas import tpu as pltpu
from jax.sharding import PartitionSpec as P

MESH = pl.DeviceIdType.MESH
LANES = 128
SLOTS = 3
ITEMS = 1 + SLOTS
ROWS = 256
HUGE = 1e30


def kernel(
    sizes,
    q_hbm,
    nk_hbm,
    nv_hbm,
    mk_hbm,
    mv_hbm,
    lists,
    o_ref,
    q_v,
    mk_v,
    mv_v,
    buf,
    far,
    prev,
    peak,
    accum,
    rows_f32,
    outgoing,
    key_tiles,
    value_tiles,
    filler,
    table,
    local_sem,
    recv_sem,
    far_sem,
    side_sem,
    far_side_sem,
    up_sem,
    down_sem,
    prev_sem,
    out_send,
    out_recv,
):
    mem_count, head_count, span_count, unit_count, list_length, group, scale = sizes
    ring = mem_count // 2
    steps = ring // 2
    row_count = q_v.shape[0]
    block_rows = row_count // head_count
    mem = lax.axis_index("mem")
    head = lax.axis_index("head")
    span = lax.axis_index("span")
    z = mem // 2
    core = mem % 2

    def device(z_at, core_at, span_at, head_at=None):
        return {
            "mem": lax.rem(z_at + ring, ring) * 2 + core_at,
            "head": head if head_at is None else head_at,
            "span": lax.rem(span_at + span_count, span_count),
        }

    loads = [
        pltpu.make_async_copy(nk_hbm, buf.at[mem, 0, 0], local_sem.at[0]),
        pltpu.make_async_copy(nv_hbm, buf.at[mem, 1, 0], local_sem.at[1]),
        pltpu.make_async_copy(mk_hbm, mk_v, local_sem.at[2]),
        pltpu.make_async_copy(mv_hbm, mv_v, local_sem.at[3]),
        pltpu.make_async_copy(q_hbm, q_v, local_sem.at[4]),
    ]
    loads[0].start()
    loads[1].start()

    barrier = pltpu.get_barrier_semaphore()
    near = [
        (dz, 0, dx)
        for dz, dx in ((1, 0), (-1, 0), (0, 1), (0, -1), (1, 1), (-1, -1), (1, -1), (-1, 1))
    ]
    near += [(0, 1, 0), (0, 1, 1), (0, 1, -1)]
    for dz, dc, dx in near:
        pl.semaphore_signal(
            barrier,
            inc=1,
            device_id=device(z + dz, core if dc == 0 else 1 - core, span + dx),
            device_id_type=MESH,
        )
    for load in loads[2:]:
        load.start()
    for dy in range(1, head_count):
        pl.semaphore_signal(
            barrier,
            inc=1,
            device_id=device(z, core, span, lax.rem(head + dy, head_count)),
            device_id_type=MESH,
        )

    def owner(entry):
        return lists[0, entry] // unit_count

    def at(z_at, core_at):
        return lax.rem(z_at + ring, ring) * 2 + core_at

    far_z = lax.rem(z + steps, ring)

    def transfer(source, item, send_sem, target, last=False):
        if last:
            landing, landed = far.at[core, :, item], far_sem.at[core, item]
        else:
            landing, landed = buf.at[source, :, item], recv_sem.at[source, item]
        return pltpu.make_async_remote_copy(
            src_ref=buf.at[source, :, item],
            dst_ref=landing,
            send_sem=send_sem,
            recv_sem=landed,
            device_id=target,
            device_id_type=MESH,
        )

    def send_up(source, item, step, last=False):
        shift = jnp.where((z == ring - 1) & (item == 0), 1, 0)
        target = device(z + 1, core, span + shift)
        return transfer(source, item, up_sem.at[step, item], target, last)

    def send_down(source, item, step, last=False):
        first = jnp.where(z > 0, 1, 0)
        later = jnp.where(z > 0, 0, -1)
        shift = jnp.where(item == 0, jnp.where(step == 0, first, later), 0)
        target = device(z - 1, core, span + shift)
        return transfer(source, item, down_sem.at[step, item], target, last)

    def send_side(source, item):
        own = source == mem
        shift = jnp.where(own & (item == 0), core, 0)
        return transfer(
            source, item, side_sem.at[source // 2, item], device(z, 1 - core, span + shift)
        )

    def far_copy(origin, item):
        return pltpu.make_async_remote_copy(
            src_ref=far.at[origin, :, item],
            dst_ref=far.at[origin, :, item],
            send_sem=far_side_sem.at[item],
            recv_sem=far_sem.at[origin, item],
            device_id=device(z, 1 - core, span),
            device_id_type=MESH,
        )

    def send_prev():
        return pltpu.make_async_remote_copy(
            src_ref=buf.at[mem, :, 0],
            dst_ref=prev,
            send_sem=prev_sem.at[0],
            recv_sem=prev_sem.at[1],
            device_id=device(z, core, span + 1),
            device_id_type=MESH,
        )

    def wait_item(source, item):
        send_side(source, item).wait_recv()

    def send_own(item):
        send_up(mem, item, 0).start()
        send_down(mem, item, 0).start()
        send_side(mem, item).start()

    owners = [owner(entry) for entry in range(list_length)]
    picks = [jnp.int32(0)] * SLOTS
    rank = jnp.int32(0)
    for entry in range(list_length):
        here = owners[entry] == mem
        for slot in range(SLOTS):
            picks[slot] = jnp.where(
                here & (rank == slot), lists[0, entry] % unit_count, picks[slot]
            )
        rank = rank + here.astype(jnp.int32)
    loads[0].wait()
    loads[1].wait()
    pl.semaphore_wait(barrier, len(near) + head_count - 1)
    send_own(0)
    send_prev().start()
    loads[2].wait()
    loads[3].wait()
    for slot in range(SLOTS):
        buf[mem, 0, 1 + slot] = mk_v[picks[slot]]
        buf[mem, 1, 1 + slot] = mv_v[picks[slot]]
    filler[...] = jnp.broadcast_to(buf[mem, 0, 0, 0:1, :], filler.shape)

    ranks = []
    for entry in range(list_length):
        same = jnp.int32(0)
        for earlier in range(entry):
            same = same + (owners[earlier] == owners[entry]).astype(jnp.int32)
        ranks.append(same)
    for item in range(1, ITEMS):
        send_own(item)
    distant = [(held // 2 == far_z).astype(jnp.int32) for held in owners]
    place_far = jnp.int32(list_length) - sum(distant)
    place_near = jnp.int32(0)
    places = []
    for entry in range(list_length):
        places.append(jnp.where(distant[entry] == 1, place_far, place_near))
        place_far = place_far + distant[entry]
        place_near = place_near + 1 - distant[entry]
    for place in range(list_length):
        code = jnp.int32(0)
        for entry in range(list_length):
            value = owners[entry] * ITEMS + 1 + ranks[entry]
            code = code + jnp.where(places[entry] == place, value, 0)
        table[place] = code
    loads[4].wait()

    def put(tile, keys, values, ones):
        tile = pl.ds(tile * LANES, LANES)
        key_tiles[tile, :] = keys
        value_tiles[tile, :LANES] = values
        value_tiles[tile, LANES:] = ones

    ones = jnp.ones((LANES, LANES), jnp.bfloat16)

    def put_chunk(tile, source, keys, values):
        used = (source < mem) | (span > 0)
        weight = jnp.full((LANES, LANES), jnp.where(used, 1.0, 0.0), jnp.float32)
        put(
            tile,
            jnp.where(used, keys, filler[...]),
            jnp.where(used, values, jnp.bfloat16(0)),
            weight.astype(jnp.bfloat16),
        )

    def put_unit(tile, place, maybe_far):
        held = table[place] // ITEMS
        item = table[place] % ITEMS
        pair = [buf[held, kind, item] for kind in range(2)]
        if maybe_far:
            there = held // 2 == far_z
            pair = [
                jnp.where(there, far[held % 2, kind, item], pair[kind]) for kind in range(2)
            ]
        put(tile, pair[0], pair[1], ones)

    def score(rows, width, masks):
        scores = lax.dot_general(
            q_v[rows, :],
            key_tiles[:width, :],
            (((1,), (1,)), ((), ())),
            preferred_element_type=jnp.float32,
        )
        if masks:
            tiles = [scores[:, t * LANES : (t + 1) * LANES] for t in range(width // LANES)]
            for t, mask in masks.items():
                tiles[t] = jnp.where(mask, tiles[t], -HUGE)
            scores = jnp.concatenate(tiles, axis=1)
        return scores

    def weigh(rows, width, scores, fresh):
        best = jnp.max(scores, axis=1, keepdims=True)
        factor = None
        if fresh:
            new_peak = jnp.broadcast_to(best, (scores.shape[0], LANES))
        else:
            old_peak = peak[rows, :]
            new_peak = jnp.maximum(old_peak, best)
            factor = jnp.exp2((old_peak - new_peak) * scale)
        wide_peak = jnp.concatenate([new_peak] * (width // LANES), axis=1)
        weights = jnp.exp2((scores - wide_peak) * scale)
        return new_peak, factor, weights.astype(jnp.bfloat16)

    def combine(rows, width, weights, factor):
        result = jnp.dot(weights, value_tiles[:width, :], preferred_element_type=jnp.float32)
        if factor is not None:
            result = accum[rows, :] * jnp.concatenate([factor, factor], axis=1) + result
        return result

    def attend_all(blocks, width, masks_of, fresh, finish):
        count = len(blocks)
        scores = score(blocks[0], width, masks_of(0))
        weighed = None
        for index in range(count + 1):
            following = None
            if index + 1 < count:
                following = score(blocks[index + 1], width, masks_of(index + 1))
            done = weighed
            if index < count:
                weighed = weigh(blocks[index], width, scores, fresh)
            if done is not None:
                new_peak, factor, weights = done
                finish(index - 1, new_peak, combine(blocks[index - 1], width, weights, factor))
            scores = following

    blocks = [pl.ds(start, ROWS) for start in range(0, row_count, ROWS)]

    def own_masks(index):
        position = (index * ROWS + lax.broadcasted_iota(jnp.int32, (ROWS, LANES), 0)) // group
        column = lax.broadcasted_iota(jnp.int32, (ROWS, LANES), 1)
        return {0: column <= position, 2: (column > position) & (span > 0)}

    def keep(index, new_peak, result):
        peak[blocks[index], :] = new_peak
        accum[blocks[index], :] = result

    beside = at(z, 1 - core)

    def begin():
        put(0, buf[mem, 0, 0], buf[mem, 1, 0], ones)
        wait_item(beside, 0)
        put_chunk(1, beside, buf[beside, 0, 0], buf[beside, 1, 0])
        send_prev().wait_recv()
        put(2, prev[0], prev[1], ones)
        attend_all(blocks, 3 * LANES, own_masks, True, keep)

    def absorb(tiles):
        attend_all(blocks, tiles * LANES, lambda index: {}, False, keep)

    @pl.loop(0, (steps - 1) * ITEMS)
    def _(tick):
        step = tick // ITEMS + 1
        item = tick % ITEMS
        turning = step == steps - 1
        below = at(z - step, core)
        wait_item(below, item)

        @pl.when(jnp.logical_not(turning))
        def _():
            send_up(below, item, step).start()

        @pl.when(turning & (item < ITEMS // 2))
        def _():
            send_up(below, item, step, True).start()

        send_side(below, item).start()
        above = at(z + step, core)
        wait_item(above, item)

        @pl.when(jnp.logical_not(turning))
        def _():
            send_down(above, item, step).start()

        @pl.when(turning & (item >= ITEMS // 2))
        def _():
            send_down(above, item, step, True).start()

        send_side(above, item).start()

        @pl.when(tick == 1)
        def _():
            begin()

        @pl.when((tick > 1) & (tick % 3 == 0))
        def _():
            reach = tick // 3
            for tile, (distance, core_at) in enumerate(
                ((-reach, core), (reach, core), (-reach, 1 - core), (reach, 1 - core))
            ):
                source = at(z + distance, core_at)
                if tile >= 2:
                    wait_item(source, 0)
                put_chunk(tile, source, buf[source, 0, 0], buf[source, 1, 0])
            absorb(4)

    early = min(list_length // 2, list_length - 2 * SLOTS)
    for item in range(1, ITEMS):
        wait_item(beside, item)

    @pl.loop(0, (steps - 1) * (ITEMS - 1))
    def _(tick):
        step = tick // (ITEMS - 1) + 1
        item = tick % (ITEMS - 1) + 1
        wait_item(at(z - step, 1 - core), item)
        wait_item(at(z + step, 1 - core), item)

    for half in range(2):
        for item in (half, half + ITEMS // 2):
            far_copy(core, item).wait_recv()
            far_copy(core, item).start()
        first, past = half * early // 2, (half + 1) * early // 2
        for place in range(first, past):
            put_unit(place - first, place, False)
        absorb(past - first)

    for item in range(ITEMS):
        far_copy(1 - core, item).wait_recv()

    def send_out(target):
        return pltpu.make_async_remote_copy(
            src_ref=outgoing.at[target],
            dst_ref=o_ref.at[:, pl.ds(pl.multiple_of(head * group * LANES, LANES), group * LANES)],
            send_sem=out_send.at[target],
            recv_sem=out_recv.at[head],
            device_id=device(z, core, span, target),
            device_id_type=MESH,
        )

    def keep_out():
        return pltpu.make_async_copy(
            outgoing.at[head],
            o_ref.at[:, pl.ds(pl.multiple_of(head * group * LANES, LANES), group * LANES)],
            out_send.at[head],
        )

    for origin in range(2):
        put_chunk(origin, far_z * 2 + origin, far[origin, 0, 0], far[origin, 1, 0])
    for place in range(early, list_length):
        put_unit(2 + place - early, place, True)
    half = head_count // 2
    hops = [half]
    for hop in range(1, half):
        hops += [half - hop, half + hop]
    hops += [0]
    targets = [lax.rem(head + hop, head_count) for hop in hops]
    parts = [
        pl.ds(pl.multiple_of(target * block_rows, block_rows), block_rows) for target in targets
    ]

    def hand_over(turn, new_peak, result):
        target = targets[turn]
        rows_f32[turn % 2] = result[:, :LANES] / result[:, LANES:]
        for member in range(group):
            part = rows_f32[turn % 2, pl.ds(member, block_rows // group, stride=group), :]
            outgoing[target, :, member * LANES : (member + 1) * LANES] = part.astype(jnp.bfloat16)
        if hops[turn] > 0:
            send_out(target).start()
        else:
            keep_out().start()

    attend_all(parts, (2 + list_length - early) * LANES, lambda turn: {}, False, hand_over)

    send_prev().wait_send()

    @pl.loop(0, (steps - 1) * ITEMS)
    def _(tick):
        step = tick // ITEMS
        item = tick % ITEMS
        send_up(at(z - step, core), item, step).wait_send()
        send_down(at(z + step, core), item, step).wait_send()
        send_side(at(z - step, core), item).wait_send()

        @pl.when(step > 0)
        def _():
            send_side(at(z + step, core), item).wait_send()

    for item in range(ITEMS // 2):
        send_up(at(z - steps + 1, core), item, steps - 1, True).wait_send()
        send_down(at(z + steps - 1, core), item + ITEMS // 2, steps - 1, True).wait_send()

    @pl.loop(0, ITEMS)
    def _(item):
        for step in (1 - steps, steps - 1):
            send_side(at(z + step, core), item).wait_send()
        far_copy(core, item).wait_send()

    keep_out().wait()

    @pl.loop(1, head_count)
    def _(hop):
        peer = lax.rem(head + hop, head_count)
        send_out(peer).wait_send()
        pltpu.make_async_remote_copy(
            src_ref=outgoing.at[peer],
            dst_ref=o_ref.at[:, pl.ds(pl.multiple_of(peer * group * LANES, LANES), group * LANES)],
            send_sem=out_send.at[peer],
            recv_sem=out_recv.at[peer],
            device_id=device(z, core, span, peer),
            device_id_type=MESH,
        ).wait_recv()


def local(query, new_keys, new_values, memory_keys, memory_values, retrieved):
    _, length, _, group, width = query.shape
    units, unit_length = memory_keys.shape[0], memory_keys.shape[1]
    mem_count = lax.axis_size("mem")
    head_count = lax.axis_size("head")
    span_count = lax.axis_size("span")
    list_length = retrieved.shape[2]
    ring = mem_count // 2
    steps = ring // 2
    rows = length * group
    tiles = 2 + max(list_length, 2 * SLOTS)
    scale = math.log2(math.e) / math.sqrt(width)
    sizes = (mem_count, head_count, span_count, units, list_length, group, scale)
    anywhere = pl.BlockSpec(memory_space=pl.ANY)
    dma = pltpu.SemaphoreType.DMA
    out = pl.pallas_call(
        functools.partial(kernel, sizes),
        out_shape=jax.ShapeDtypeStruct(
            (length // head_count, head_count * group * width), jnp.bfloat16
        ),
        in_specs=[anywhere] * 5 + [pl.BlockSpec(memory_space=pltpu.SMEM)],
        out_specs=anywhere,
        scratch_shapes=[
            pltpu.VMEM((rows, width), jnp.bfloat16),
            pltpu.VMEM((units, unit_length, width), jnp.bfloat16),
            pltpu.VMEM((units, unit_length, width), jnp.bfloat16),
            pltpu.VMEM((mem_count, 2, ITEMS, unit_length, width), jnp.bfloat16),
            pltpu.VMEM((2, 2, ITEMS, unit_length, width), jnp.bfloat16),
            pltpu.VMEM((2, length, width), jnp.bfloat16),
            pltpu.VMEM((rows, LANES), jnp.float32),
            pltpu.VMEM((rows, 2 * LANES), jnp.float32),
            pltpu.VMEM((2, rows // head_count, width), jnp.float32),
            pltpu.VMEM((head_count, length // head_count, group * width), jnp.bfloat16),
            pltpu.VMEM((tiles * unit_length, width), jnp.bfloat16),
            pltpu.VMEM((tiles * unit_length, 2 * width), jnp.bfloat16),
            pltpu.VMEM((unit_length, width), jnp.bfloat16),
            pltpu.SMEM((list_length,), jnp.int32),
            dma((5,)),
            dma((mem_count, ITEMS)),
            dma((2, ITEMS)),
            dma((ring, ITEMS)),
            dma((ITEMS,)),
            dma((steps, ITEMS)),
            dma((steps, ITEMS)),
            dma((2,)),
            dma((head_count,)),
            dma((head_count,)),
        ],
        compiler_params=pltpu.CompilerParams(
            collective_id=0, has_side_effects=True, vmem_limit_bytes=62 * 1024 * 1024
        ),
    )(
        query.reshape(rows, width),
        new_keys.reshape(length, width),
        new_values.reshape(length, width),
        memory_keys.reshape(units, unit_length, width),
        memory_values.reshape(units, unit_length, width),
        retrieved.reshape(1, list_length),
    )
    return out[None]


def solution(mesh):
    return jax.shard_map(
        local,
        mesh=mesh,
        in_specs=(
            P("span", "mem", "head", None, None),
            P("span", "mem", "head", None),
            P("span", "mem", "head", None),
            P("mem", None, "head", None),
            P("mem", None, "head", None),
            P("span", "head", None),
        ),
        out_specs=P("span", ("mem", "head"), None),
        check_vma=False,
    )
```

```python
import functools
import math

import jax
import jax.numpy as jnp
from jax import lax
from jax.experimental import pallas as pl
from jax.experimental.pallas import tpu as pltpu
from jax.sharding import PartitionSpec as P

MESH = pl.DeviceIdType.MESH
LANES = 128
SLOTS = 3
ITEMS = 1 + SLOTS
ROWS = 256
HUGE = 1e30


def kernel(
    sizes,
    q_hbm,
    nk_hbm,
    nv_hbm,
    mk_hbm,
    mv_hbm,
    lists_hbm,
    o_ref,
    q_v,
    mk_v,
    mv_v,
    buf,
    far,
    prev,
    peak,
    accum,
    rows_f32,
    outgoing,
    key_tiles,
    value_tiles,
    filler,
    table,
    lists,
    local_sem,
    recv_sem,
    far_sem,
    side_sem,
    far_side_sem,
    up_sem,
    down_sem,
    prev_sem,
    out_send,
    out_recv,
    word_sem,
):
    mem_count, head_count, span_count, unit_count, list_length, group, scale = sizes
    ring = mem_count // 2
    steps = ring // 2
    row_count = q_v.shape[0]
    block_rows = row_count // head_count
    mem = lax.axis_index("mem")
    head = lax.axis_index("head")
    span = lax.axis_index("span")
    z = mem // 2
    core = mem % 2

    def device(z_at, core_at, span_at, head_at=None):
        return {
            "mem": lax.rem(z_at + ring, ring) * 2 + core_at,
            "head": head if head_at is None else head_at,
            "span": lax.rem(span_at + span_count, span_count),
        }

    loads = [
        pltpu.make_async_copy(nk_hbm, buf.at[mem, 0, 0], local_sem.at[0]),
        pltpu.make_async_copy(nv_hbm, buf.at[mem, 1, 0], local_sem.at[1]),
        pltpu.make_async_copy(mk_hbm, mk_v, local_sem.at[2]),
        pltpu.make_async_copy(mv_hbm, mv_v, local_sem.at[3]),
        pltpu.make_async_copy(q_hbm, q_v, local_sem.at[4]),
        pltpu.make_async_copy(lists_hbm, lists, local_sem.at[5]),
    ]
    loads[0].start()
    loads[1].start()
    loads[5].start()

    barrier = pltpu.get_barrier_semaphore()
    near = [
        (dz, 0, dx)
        for dz, dx in ((1, 0), (-1, 0), (0, 1), (0, -1), (1, 1), (-1, -1), (1, -1), (-1, 1))
    ]
    near += [(0, 1, 0), (0, 1, 1), (0, 1, -1)]
    for dz, dc, dx in near:
        pl.semaphore_signal(
            barrier,
            inc=1,
            device_id=device(z + dz, core if dc == 0 else 1 - core, span + dx),
            device_id_type=MESH,
        )
    for load in loads[2:5]:
        load.start()
    beyond = [lax.rem(head + hop, head_count) for hop in (1, head_count - 1)]
    for head_at in beyond:
        pl.semaphore_signal(
            barrier, inc=1, device_id=device(z, core, span, head_at), device_id_type=MESH
        )

    rounds = head_count // 2 - 1

    def tell(turn):
        for way, head_at in enumerate(beyond):
            pl.semaphore_signal(
                word_sem.at[way, turn],
                inc=1,
                device_id=device(z, core, span, head_at),
                device_id_type=MESH,
            )

    def hear(turn):
        for way in range(2):
            pl.semaphore_wait(word_sem.at[way, turn], 1)

    def owner(entry):
        return lists[0, entry] // unit_count

    def at(z_at, core_at):
        return lax.rem(z_at + ring, ring) * 2 + core_at

    far_z = lax.rem(z + steps, ring)

    def transfer(source, item, send_sem, target, last=False):
        if last:
            landing, landed = far.at[core, :, item], far_sem.at[core, item]
        else:
            landing, landed = buf.at[source, :, item], recv_sem.at[source, item]
        return pltpu.make_async_remote_copy(
            src_ref=buf.at[source, :, item],
            dst_ref=landing,
            send_sem=send_sem,
            recv_sem=landed,
            device_id=target,
            device_id_type=MESH,
        )

    def send_up(source, item, step, last=False):
        shift = jnp.where((z == ring - 1) & (item == 0), 1, 0)
        target = device(z + 1, core, span + shift)
        return transfer(source, item, up_sem.at[step, item], target, last)

    def send_down(source, item, step, last=False):
        first = jnp.where(z > 0, 1, 0)
        later = jnp.where(z > 0, 0, -1)
        shift = jnp.where(item == 0, jnp.where(step == 0, first, later), 0)
        target = device(z - 1, core, span + shift)
        return transfer(source, item, down_sem.at[step, item], target, last)

    def send_side(source, item):
        own = source == mem
        shift = jnp.where(own & (item == 0), core, 0)
        return transfer(
            source, item, side_sem.at[source // 2, item], device(z, 1 - core, span + shift)
        )

    def far_copy(origin, item):
        return pltpu.make_async_remote_copy(
            src_ref=far.at[origin, :, item],
            dst_ref=far.at[origin, :, item],
            send_sem=far_side_sem.at[item],
            recv_sem=far_sem.at[origin, item],
            device_id=device(z, 1 - core, span),
            device_id_type=MESH,
        )

    def send_prev():
        return pltpu.make_async_remote_copy(
            src_ref=buf.at[mem, :, 0],
            dst_ref=prev,
            send_sem=prev_sem.at[0],
            recv_sem=prev_sem.at[1],
            device_id=device(z, core, span + 1),
            device_id_type=MESH,
        )

    def wait_item(source, item):
        send_side(source, item).wait_recv()

    def send_own(item):
        send_up(mem, item, 0).start()
        send_down(mem, item, 0).start()
        send_side(mem, item).start()

    loads[5].wait()
    owners = [owner(entry) for entry in range(list_length)]
    picks = [jnp.int32(0)] * SLOTS
    rank = jnp.int32(0)
    for entry in range(list_length):
        here = owners[entry] == mem
        for slot in range(SLOTS):
            picks[slot] = jnp.where(
                here & (rank == slot), lists[0, entry] % unit_count, picks[slot]
            )
        rank = rank + here.astype(jnp.int32)
    loads[0].wait()
    loads[1].wait()
    pl.semaphore_wait(barrier, len(near) + 2)
    send_own(0)
    send_prev().start()
    loads[2].wait()
    loads[3].wait()
    for slot in range(SLOTS):
        buf[mem, 0, 1 + slot] = mk_v[picks[slot]]
        buf[mem, 1, 1 + slot] = mv_v[picks[slot]]
    filler[...] = jnp.broadcast_to(buf[mem, 0, 0, 0:1, :], filler.shape)

    ranks = []
    for entry in range(list_length):
        same = jnp.int32(0)
        for earlier in range(entry):
            same = same + (owners[earlier] == owners[entry]).astype(jnp.int32)
        ranks.append(same)
    for item in range(1, ITEMS):
        send_own(item)
    if rounds > 0:
        tell(0)
    distant = [(held // 2 == far_z).astype(jnp.int32) for held in owners]
    place_far = jnp.int32(list_length) - sum(distant)
    place_near = jnp.int32(0)
    places = []
    for entry in range(list_length):
        places.append(jnp.where(distant[entry] == 1, place_far, place_near))
        place_far = place_far + distant[entry]
        place_near = place_near + 1 - distant[entry]
    for place in range(list_length):
        code = jnp.int32(0)
        for entry in range(list_length):
            value = owners[entry] * ITEMS + 1 + ranks[entry]
            code = code + jnp.where(places[entry] == place, value, 0)
        table[place] = code
    loads[4].wait()

    def put(tile, keys, values, ones):
        tile = pl.ds(tile * LANES, LANES)
        key_tiles[tile, :] = keys
        value_tiles[tile, :LANES] = values
        value_tiles[tile, LANES:] = ones

    ones = jnp.ones((LANES, LANES), jnp.bfloat16)

    def put_chunk(tile, source, keys, values):
        used = (source < mem) | (span > 0)
        weight = jnp.full((LANES, LANES), jnp.where(used, 1.0, 0.0), jnp.float32)
        put(
            tile,
            jnp.where(used, keys, filler[...]),
            jnp.where(used, values, jnp.bfloat16(0)),
            weight.astype(jnp.bfloat16),
        )

    def put_unit(tile, place, maybe_far):
        held = table[place] // ITEMS
        item = table[place] % ITEMS
        pair = [buf[held, kind, item] for kind in range(2)]
        if maybe_far:
            there = held // 2 == far_z
            pair = [
                jnp.where(there, far[held % 2, kind, item], pair[kind]) for kind in range(2)
            ]
        put(tile, pair[0], pair[1], ones)

    def score(rows, width, masks):
        scores = lax.dot_general(
            q_v[rows, :],
            key_tiles[:width, :],
            (((1,), (1,)), ((), ())),
            preferred_element_type=jnp.float32,
        )
        if masks:
            tiles = [scores[:, t * LANES : (t + 1) * LANES] for t in range(width // LANES)]
            for t, mask in masks.items():
                tiles[t] = jnp.where(mask, tiles[t], -HUGE)
            scores = jnp.concatenate(tiles, axis=1)
        return scores

    def weigh(rows, width, scores, fresh):
        best = jnp.max(scores, axis=1, keepdims=True)
        factor = None
        if fresh:
            new_peak = jnp.broadcast_to(best, (scores.shape[0], LANES))
        else:
            old_peak = peak[rows, :]
            new_peak = jnp.maximum(old_peak, best)
            factor = jnp.exp2((old_peak - new_peak) * scale)
        wide_peak = jnp.concatenate([new_peak] * (width // LANES), axis=1)
        weights = jnp.exp2((scores - wide_peak) * scale)
        return new_peak, factor, weights.astype(jnp.bfloat16)

    def combine(rows, width, weights, factor):
        result = jnp.dot(weights, value_tiles[:width, :], preferred_element_type=jnp.float32)
        if factor is not None:
            result = accum[rows, :] * jnp.concatenate([factor, factor], axis=1) + result
        return result

    def attend_all(blocks, width, masks_of, fresh, finish):
        count = len(blocks)
        scores = score(blocks[0], width, masks_of(0))
        weighed = None
        for index in range(count + 1):
            following = None
            if index + 1 < count:
                following = score(blocks[index + 1], width, masks_of(index + 1))
            done = weighed
            if index < count:
                weighed = weigh(blocks[index], width, scores, fresh)
            if done is not None:
                new_peak, factor, weights = done
                finish(index - 1, new_peak, combine(blocks[index - 1], width, weights, factor))
            scores = following

    blocks = [pl.ds(start, ROWS) for start in range(0, row_count, ROWS)]

    def own_masks(index):
        position = (index * ROWS + lax.broadcasted_iota(jnp.int32, (ROWS, LANES), 0)) // group
        column = lax.broadcasted_iota(jnp.int32, (ROWS, LANES), 1)
        return {0: column <= position, 2: (column > position) & (span > 0)}

    def keep(index, new_peak, result):
        peak[blocks[index], :] = new_peak
        accum[blocks[index], :] = result

    beside = at(z, 1 - core)

    def begin():
        put(0, buf[mem, 0, 0], buf[mem, 1, 0], ones)
        wait_item(beside, 0)
        put_chunk(1, beside, buf[beside, 0, 0], buf[beside, 1, 0])
        send_prev().wait_recv()
        put(2, prev[0], prev[1], ones)
        attend_all(blocks, 3 * LANES, own_masks, True, keep)

    def absorb(tiles):
        attend_all(blocks, tiles * LANES, lambda index: {}, False, keep)

    @pl.loop(0, (steps - 1) * ITEMS)
    def _(tick):
        step = tick // ITEMS + 1
        item = tick % ITEMS
        turning = step == steps - 1
        below = at(z - step, core)
        wait_item(below, item)

        @pl.when(jnp.logical_not(turning))
        def _():
            send_up(below, item, step).start()

        @pl.when(turning & (item < ITEMS // 2))
        def _():
            send_up(below, item, step, True).start()

        send_side(below, item).start()
        above = at(z + step, core)
        wait_item(above, item)

        @pl.when(jnp.logical_not(turning))
        def _():
            send_down(above, item, step).start()

        @pl.when(turning & (item >= ITEMS // 2))
        def _():
            send_down(above, item, step, True).start()

        send_side(above, item).start()

        for turn in range(1, rounds):

            @pl.when(tick == turn * ITEMS)
            def _():
                hear(turn - 1)
                tell(turn)

        @pl.when(tick == 1)
        def _():
            begin()

        @pl.when((tick > 1) & (tick % 3 == 0))
        def _():
            reach = tick // 3
            for tile, (distance, core_at) in enumerate(
                ((-reach, core), (reach, core), (-reach, 1 - core), (reach, 1 - core))
            ):
                source = at(z + distance, core_at)
                if tile >= 2:
                    wait_item(source, 0)
                put_chunk(tile, source, buf[source, 0, 0], buf[source, 1, 0])
            absorb(4)

    early = min(list_length // 2, list_length - 2 * SLOTS)
    for item in range(1, ITEMS):
        wait_item(beside, item)

    @pl.loop(0, (steps - 1) * (ITEMS - 1))
    def _(tick):
        step = tick // (ITEMS - 1) + 1
        item = tick % (ITEMS - 1) + 1
        wait_item(at(z - step, 1 - core), item)
        wait_item(at(z + step, 1 - core), item)

    for half in range(2):
        for item in (half, half + ITEMS // 2):
            far_copy(core, item).wait_recv()
            far_copy(core, item).start()
        first, past = half * early // 2, (half + 1) * early // 2
        for place in range(first, past):
            put_unit(place - first, place, False)
        absorb(past - first)

    if rounds > 0:
        hear(rounds - 1)
    for item in range(ITEMS):
        far_copy(1 - core, item).wait_recv()

    def send_out(target):
        return pltpu.make_async_remote_copy(
            src_ref=outgoing.at[target],
            dst_ref=o_ref.at[:, pl.ds(pl.multiple_of(head * group * LANES, LANES), group * LANES)],
            send_sem=out_send.at[target],
            recv_sem=out_recv.at[head],
            device_id=device(z, core, span, target),
            device_id_type=MESH,
        )

    def keep_out():
        return pltpu.make_async_copy(
            outgoing.at[head],
            o_ref.at[:, pl.ds(pl.multiple_of(head * group * LANES, LANES), group * LANES)],
            out_send.at[head],
        )

    for origin in range(2):
        put_chunk(origin, far_z * 2 + origin, far[origin, 0, 0], far[origin, 1, 0])
    for place in range(early, list_length):
        put_unit(2 + place - early, place, True)
    half = head_count // 2
    hops = [half]
    for hop in range(1, half):
        hops += [half - hop, half + hop]
    hops += [0]
    targets = [lax.rem(head + hop, head_count) for hop in hops]
    parts = [
        pl.ds(pl.multiple_of(target * block_rows, block_rows), block_rows) for target in targets
    ]

    def hand_over(turn, new_peak, result):
        target = targets[turn]
        rows_f32[turn % 2] = result[:, :LANES] / result[:, LANES:]
        for member in range(group):
            part = rows_f32[turn % 2, pl.ds(member, block_rows // group, stride=group), :]
            outgoing[target, :, member * LANES : (member + 1) * LANES] = part.astype(jnp.bfloat16)
        if hops[turn] > 0:
            send_out(target).start()
        else:
            keep_out().start()

    attend_all(parts, (2 + list_length - early) * LANES, lambda turn: {}, False, hand_over)

    send_prev().wait_send()

    @pl.loop(0, (steps - 1) * ITEMS)
    def _(tick):
        step = tick // ITEMS
        item = tick % ITEMS
        send_up(at(z - step, core), item, step).wait_send()
        send_down(at(z + step, core), item, step).wait_send()
        send_side(at(z - step, core), item).wait_send()

        @pl.when(step > 0)
        def _():
            send_side(at(z + step, core), item).wait_send()

    for item in range(ITEMS // 2):
        send_up(at(z - steps + 1, core), item, steps - 1, True).wait_send()
        send_down(at(z + steps - 1, core), item + ITEMS // 2, steps - 1, True).wait_send()

    @pl.loop(0, ITEMS)
    def _(item):
        for step in (1 - steps, steps - 1):
            send_side(at(z + step, core), item).wait_send()
        far_copy(core, item).wait_send()

    keep_out().wait()

    @pl.loop(1, head_count)
    def _(hop):
        peer = lax.rem(head + hop, head_count)
        send_out(peer).wait_send()
        pltpu.make_async_remote_copy(
            src_ref=outgoing.at[peer],
            dst_ref=o_ref.at[:, pl.ds(pl.multiple_of(peer * group * LANES, LANES), group * LANES)],
            send_sem=out_send.at[peer],
            recv_sem=out_recv.at[peer],
            device_id=device(z, core, span, peer),
            device_id_type=MESH,
        ).wait_recv()


def local(query, new_keys, new_values, memory_keys, memory_values, retrieved):
    _, length, _, group, width = query.shape
    units, unit_length = memory_keys.shape[0], memory_keys.shape[1]
    mem_count = lax.axis_size("mem")
    head_count = lax.axis_size("head")
    span_count = lax.axis_size("span")
    list_length = retrieved.shape[2]
    ring = mem_count // 2
    steps = ring // 2
    rows = length * group
    tiles = 2 + max(list_length, 2 * SLOTS)
    scale = math.log2(math.e) / math.sqrt(width)
    sizes = (mem_count, head_count, span_count, units, list_length, group, scale)
    anywhere = pl.BlockSpec(memory_space=pl.ANY)
    dma = pltpu.SemaphoreType.DMA
    out = pl.pallas_call(
        functools.partial(kernel, sizes),
        out_shape=jax.ShapeDtypeStruct(
            (length // head_count, head_count * group * width), jnp.bfloat16
        ),
        in_specs=[anywhere] * 6,
        out_specs=anywhere,
        scratch_shapes=[
            pltpu.VMEM((rows, width), jnp.bfloat16),
            pltpu.VMEM((units, unit_length, width), jnp.bfloat16),
            pltpu.VMEM((units, unit_length, width), jnp.bfloat16),
            pltpu.VMEM((mem_count, 2, ITEMS, unit_length, width), jnp.bfloat16),
            pltpu.VMEM((2, 2, ITEMS, unit_length, width), jnp.bfloat16),
            pltpu.VMEM((2, length, width), jnp.bfloat16),
            pltpu.VMEM((rows, LANES), jnp.float32),
            pltpu.VMEM((rows, 2 * LANES), jnp.float32),
            pltpu.VMEM((2, rows // head_count, width), jnp.float32),
            pltpu.VMEM((head_count, length // head_count, group * width), jnp.bfloat16),
            pltpu.VMEM((tiles * unit_length, width), jnp.bfloat16),
            pltpu.VMEM((tiles * unit_length, 2 * width), jnp.bfloat16),
            pltpu.VMEM((unit_length, width), jnp.bfloat16),
            pltpu.SMEM((list_length,), jnp.int32),
            pltpu.SMEM((1, list_length), jnp.int32),
            dma((6,)),
            dma((mem_count, ITEMS)),
            dma((2, ITEMS)),
            dma((ring, ITEMS)),
            dma((ITEMS,)),
            dma((steps, ITEMS)),
            dma((steps, ITEMS)),
            dma((2,)),
            dma((head_count,)),
            dma((head_count,)),
            pltpu.SemaphoreType.REGULAR((2, max(1, head_count // 2 - 1))),
        ],
        compiler_params=pltpu.CompilerParams(
            collective_id=0, has_side_effects=True, vmem_limit_bytes=62 * 1024 * 1024
        ),
    )(
        query.reshape(rows, width),
        new_keys.reshape(length, width),
        new_values.reshape(length, width),
        memory_keys.reshape(units, unit_length, width),
        memory_values.reshape(units, unit_length, width),
        retrieved.reshape(1, list_length),
    )
    return out[None]


def solution(mesh):
    return jax.shard_map(
        local,
        mesh=mesh,
        in_specs=(
            P("span", "mem", "head", None, None),
            P("span", "mem", "head", None),
            P("span", "mem", "head", None),
            P("mem", None, "head", None),
            P("mem", None, "head", None),
            P("span", "head", None),
        ),
        out_specs=P("span", ("mem", "head"), None),
        check_vma=False,
    )
```

```python
import functools
import math

import jax
import jax.numpy as jnp
from jax import lax
from jax.experimental import pallas as pl
from jax.experimental.pallas import tpu as pltpu
from jax.sharding import PartitionSpec as P

MESH = pl.DeviceIdType.MESH
LANES = 128
SLOTS = 3
ITEMS = 1 + SLOTS
ROWS = 256
HUGE = 1e30


def kernel(
    sizes,
    q_hbm,
    nk_hbm,
    nv_hbm,
    mk_hbm,
    mv_hbm,
    lists_hbm,
    o_ref,
    q_v,
    mk_v,
    mv_v,
    buf,
    far,
    prev,
    peak,
    accum,
    rows_f32,
    outgoing,
    key_tiles,
    value_tiles,
    filler,
    table,
    lists,
    local_sem,
    recv_sem,
    far_sem,
    side_sem,
    far_side_sem,
    up_sem,
    down_sem,
    prev_sem,
    out_send,
    out_recv,
    word_sem,
):
    mem_count, head_count, span_count, unit_count, list_length, group, scale = sizes
    ring = mem_count // 2
    steps = ring // 2
    row_count = q_v.shape[0]
    block_rows = row_count // head_count
    mem = lax.axis_index("mem")
    head = lax.axis_index("head")
    span = lax.axis_index("span")
    z = mem // 2
    core = mem % 2

    def device(z_at, core_at, span_at, head_at=None):
        return {
            "mem": lax.rem(z_at + ring, ring) * 2 + core_at,
            "head": head if head_at is None else head_at,
            "span": lax.rem(span_at + span_count, span_count),
        }

    loads = [
        pltpu.make_async_copy(nk_hbm, buf.at[mem, 0, 0], local_sem.at[0]),
        pltpu.make_async_copy(nv_hbm, buf.at[mem, 1, 0], local_sem.at[1]),
        pltpu.make_async_copy(mk_hbm, mk_v, local_sem.at[2]),
        pltpu.make_async_copy(mv_hbm, mv_v, local_sem.at[3]),
        pltpu.make_async_copy(q_hbm, q_v, local_sem.at[4]),
        pltpu.make_async_copy(lists_hbm, lists, local_sem.at[5]),
    ]
    loads[0].start()
    loads[1].start()
    loads[5].start()

    barrier = pltpu.get_barrier_semaphore()
    near = [
        (dz, 0, dx)
        for dz, dx in ((1, 0), (-1, 0), (0, 1), (0, -1), (1, 1), (-1, -1), (1, -1), (-1, 1))
    ]
    near += [(0, 1, 0), (0, 1, 1), (0, 1, -1)]
    for dz, dc, dx in near:
        pl.semaphore_signal(
            barrier,
            inc=1,
            device_id=device(z + dz, core if dc == 0 else 1 - core, span + dx),
            device_id_type=MESH,
        )
    for load in loads[2:5]:
        load.start()
    beyond = [lax.rem(head + hop, head_count) for hop in (1, head_count - 1)]
    for head_at in beyond:
        pl.semaphore_signal(
            barrier, inc=1, device_id=device(z, core, span, head_at), device_id_type=MESH
        )

    rounds = head_count // 2 - 1

    def tell(turn):
        for way, head_at in enumerate(beyond):
            pl.semaphore_signal(
                word_sem.at[way, turn],
                inc=1,
                device_id=device(z, core, span, head_at),
                device_id_type=MESH,
            )

    def hear(turn):
        for way in range(2):
            pl.semaphore_wait(word_sem.at[way, turn], 1)

    def owner(entry):
        return lists[0, entry] // unit_count

    def at(z_at, core_at):
        return lax.rem(z_at + ring, ring) * 2 + core_at

    far_z = lax.rem(z + steps, ring)

    def transfer(source, item, send_sem, target, last=False):
        if last:
            landing, landed = far.at[core, :, item], far_sem.at[core, item]
        else:
            landing, landed = buf.at[source, :, item], recv_sem.at[source, item]
        return pltpu.make_async_remote_copy(
            src_ref=buf.at[source, :, item],
            dst_ref=landing,
            send_sem=send_sem,
            recv_sem=landed,
            device_id=target,
            device_id_type=MESH,
        )

    def send_up(source, item, step, last=False):
        shift = jnp.where((z == ring - 1) & (item == 0), 1, 0)
        target = device(z + 1, core, span + shift)
        return transfer(source, item, up_sem.at[step, item], target, last)

    def send_down(source, item, step, last=False):
        first = jnp.where(z > 0, 1, 0)
        later = jnp.where(z > 0, 0, -1)
        shift = jnp.where(item == 0, jnp.where(step == 0, first, later), 0)
        target = device(z - 1, core, span + shift)
        return transfer(source, item, down_sem.at[step, item], target, last)

    def send_side(source, item):
        own = source == mem
        shift = jnp.where(own & (item == 0), core, 0)
        return transfer(
            source, item, side_sem.at[source // 2, item], device(z, 1 - core, span + shift)
        )

    def far_copy(origin, item):
        return pltpu.make_async_remote_copy(
            src_ref=far.at[origin, :, item],
            dst_ref=far.at[origin, :, item],
            send_sem=far_side_sem.at[item],
            recv_sem=far_sem.at[origin, item],
            device_id=device(z, 1 - core, span),
            device_id_type=MESH,
        )

    def send_prev():
        return pltpu.make_async_remote_copy(
            src_ref=buf.at[mem, :, 0],
            dst_ref=prev,
            send_sem=prev_sem.at[0],
            recv_sem=prev_sem.at[1],
            device_id=device(z, core, span + 1),
            device_id_type=MESH,
        )

    def wait_item(source, item):
        send_side(source, item).wait_recv()

    def send_own(item):
        send_up(mem, item, 0).start()
        send_down(mem, item, 0).start()
        send_side(mem, item).start()

    loads[5].wait()
    owners = [owner(entry) for entry in range(list_length)]
    picks = [jnp.int32(0)] * SLOTS
    rank = jnp.int32(0)
    for entry in range(list_length):
        here = owners[entry] == mem
        for slot in range(SLOTS):
            picks[slot] = jnp.where(
                here & (rank == slot), lists[0, entry] % unit_count, picks[slot]
            )
        rank = rank + here.astype(jnp.int32)
    loads[0].wait()
    loads[1].wait()
    pl.semaphore_wait(barrier, len(near) + 2)
    send_own(0)
    send_prev().start()
    loads[2].wait()
    loads[3].wait()
    for slot in range(SLOTS):
        buf[mem, 0, 1 + slot] = mk_v[picks[slot]]
        buf[mem, 1, 1 + slot] = mv_v[picks[slot]]
    filler[...] = jnp.broadcast_to(buf[mem, 0, 0, 0:1, :], filler.shape)

    ranks = []
    for entry in range(list_length):
        same = jnp.int32(0)
        for earlier in range(entry):
            same = same + (owners[earlier] == owners[entry]).astype(jnp.int32)
        ranks.append(same)
    for item in range(1, ITEMS):
        send_own(item)
    if rounds > 0:
        tell(0)
    distant = [(held // 2 == far_z).astype(jnp.int32) for held in owners]
    place_far = jnp.int32(list_length) - sum(distant)
    place_near = jnp.int32(0)
    places = []
    for entry in range(list_length):
        places.append(jnp.where(distant[entry] == 1, place_far, place_near))
        place_far = place_far + distant[entry]
        place_near = place_near + 1 - distant[entry]
    for place in range(list_length):
        code = jnp.int32(0)
        for entry in range(list_length):
            value = owners[entry] * ITEMS + 1 + ranks[entry]
            code = code + jnp.where(places[entry] == place, value, 0)
        table[place] = code
    loads[4].wait()

    def put(tile, keys, values, ones):
        tile = pl.ds(tile * LANES, LANES)
        key_tiles[tile, :] = keys
        value_tiles[tile, :LANES] = values
        value_tiles[tile, LANES:] = ones

    ones = jnp.ones((LANES, LANES), jnp.bfloat16)

    def put_chunk(tile, source, keys, values):
        used = (source < mem) | (span > 0)
        weight = jnp.full((LANES, LANES), jnp.where(used, 1.0, 0.0), jnp.float32)
        put(
            tile,
            jnp.where(used, keys, filler[...]),
            jnp.where(used, values, jnp.bfloat16(0)),
            weight.astype(jnp.bfloat16),
        )

    def put_unit(tile, place, maybe_far):
        held = table[place] // ITEMS
        item = table[place] % ITEMS
        pair = [buf[held, kind, item] for kind in range(2)]
        if maybe_far:
            there = held // 2 == far_z
            pair = [
                jnp.where(there, far[held % 2, kind, item], pair[kind]) for kind in range(2)
            ]
        put(tile, pair[0], pair[1], ones)

    def score(rows, width, masks):
        scores = lax.dot_general(
            q_v[rows, :],
            key_tiles[:width, :],
            (((1,), (1,)), ((), ())),
            preferred_element_type=jnp.float32,
        )
        if masks:
            tiles = [scores[:, t * LANES : (t + 1) * LANES] for t in range(width // LANES)]
            for t, mask in masks.items():
                tiles[t] = jnp.where(mask, tiles[t], -HUGE)
            scores = jnp.concatenate(tiles, axis=1)
        return scores

    def weigh(rows, width, scores, fresh):
        best = jnp.max(scores, axis=1, keepdims=True)
        factor = None
        if fresh:
            new_peak = jnp.broadcast_to(best, (scores.shape[0], LANES))
        else:
            old_peak = peak[rows, :]
            new_peak = jnp.maximum(old_peak, best)
            factor = jnp.exp2((old_peak - new_peak) * scale)
        wide_peak = jnp.concatenate([new_peak] * (width // LANES), axis=1)
        weights = jnp.exp2((scores - wide_peak) * scale)
        return new_peak, factor, weights.astype(jnp.bfloat16)

    def combine(rows, width, weights, factor):
        result = jnp.dot(weights, value_tiles[:width, :], preferred_element_type=jnp.float32)
        if factor is not None:
            result = accum[rows, :] * jnp.concatenate([factor, factor], axis=1) + result
        return result

    def attend_all(blocks, width, masks_of, fresh, finish):
        count = len(blocks)
        scores = score(blocks[0], width, masks_of(0))
        weighed = None
        for index in range(count + 1):
            following = None
            if index + 1 < count:
                following = score(blocks[index + 1], width, masks_of(index + 1))
            done = weighed
            if index < count:
                weighed = weigh(blocks[index], width, scores, fresh)
            if done is not None:
                new_peak, factor, weights = done
                finish(index - 1, new_peak, combine(blocks[index - 1], width, weights, factor))
            scores = following

    blocks = [pl.ds(start, ROWS) for start in range(0, row_count, ROWS)]

    def own_masks(index):
        position = (index * ROWS + lax.broadcasted_iota(jnp.int32, (ROWS, LANES), 0)) // group
        column = lax.broadcasted_iota(jnp.int32, (ROWS, LANES), 1)
        return {0: column <= position, 2: (column > position) & (span > 0)}

    def keep(index, new_peak, result):
        peak[blocks[index], :] = new_peak
        accum[blocks[index], :] = result

    beside = at(z, 1 - core)

    def begin():
        put(0, buf[mem, 0, 0], buf[mem, 1, 0], ones)
        wait_item(beside, 0)
        put_chunk(1, beside, buf[beside, 0, 0], buf[beside, 1, 0])
        send_prev().wait_recv()
        put(2, prev[0], prev[1], ones)
        attend_all(blocks, 3 * LANES, own_masks, True, keep)

    def absorb(tiles):
        attend_all(blocks, tiles * LANES, lambda index: {}, False, keep)

    @pl.loop(0, (steps - 1) * ITEMS)
    def _(tick):
        step = tick // ITEMS + 1
        item = tick % ITEMS
        turning = step == steps - 1
        below = at(z - step, core)
        wait_item(below, item)

        @pl.when(jnp.logical_not(turning))
        def _():
            send_up(below, item, step).start()

        @pl.when(turning & (item < ITEMS // 2))
        def _():
            send_up(below, item, step, True).start()

        send_side(below, item).start()
        above = at(z + step, core)
        wait_item(above, item)

        @pl.when(jnp.logical_not(turning))
        def _():
            send_down(above, item, step).start()

        @pl.when(turning & (item >= ITEMS // 2))
        def _():
            send_down(above, item, step, True).start()

        send_side(above, item).start()

        for turn in range(1, rounds):

            @pl.when(tick == turn * ITEMS)
            def _():
                hear(turn - 1)
                tell(turn)

        @pl.when(tick == 1)
        def _():
            begin()

        @pl.when((tick > 1) & (tick % 3 == 0))
        def _():
            reach = tick // 3
            for tile, (distance, core_at) in enumerate(
                ((-reach, core), (reach, core), (-reach, 1 - core), (reach, 1 - core))
            ):
                source = at(z + distance, core_at)
                if tile >= 2:
                    wait_item(source, 0)
                put_chunk(tile, source, buf[source, 0, 0], buf[source, 1, 0])
            absorb(4)

    sure = list_length - 2 * SLOTS
    early = min(3 * list_length // 8, sure) // 2 * 2
    for item in range(1, ITEMS):
        wait_item(beside, item)

    @pl.loop(0, (steps - 1) * (ITEMS - 1))
    def _(tick):
        step = tick // (ITEMS - 1) + 1
        item = tick % (ITEMS - 1) + 1
        wait_item(at(z - step, 1 - core), item)
        wait_item(at(z + step, 1 - core), item)

    def put_early(first, past):
        for place in range(first, past):
            put_unit(place - first, place, False)

    split = min(ITEMS, early)
    put_early(0, split)
    for half in range(2):
        for item in (half, half + ITEMS // 2):
            far_copy(core, item).wait_recv()
            far_copy(core, item).start()
        if half == 0:
            absorb(split)
        elif early > split:
            put_early(split, early)
            absorb(early - split)

    if rounds > 0:
        hear(rounds - 1)
    for place in range(early, sure):
        put_unit(2 + place - early, place, False)
    for item in range(ITEMS):
        far_copy(1 - core, item).wait_recv()

    def send_out(target):
        return pltpu.make_async_remote_copy(
            src_ref=outgoing.at[target],
            dst_ref=o_ref.at[:, pl.ds(pl.multiple_of(head * group * LANES, LANES), group * LANES)],
            send_sem=out_send.at[target],
            recv_sem=out_recv.at[head],
            device_id=device(z, core, span, target),
            device_id_type=MESH,
        )

    def keep_out():
        return pltpu.make_async_copy(
            outgoing.at[head],
            o_ref.at[:, pl.ds(pl.multiple_of(head * group * LANES, LANES), group * LANES)],
            out_send.at[head],
        )

    for origin in range(2):
        put_chunk(origin, far_z * 2 + origin, far[origin, 0, 0], far[origin, 1, 0])
    for place in range(sure, list_length):
        put_unit(2 + place - early, place, True)
    half = head_count // 2
    hops = [half]
    for hop in range(1, half):
        hops += [half - hop, half + hop]
    hops += [0]
    targets = [lax.rem(head + hop, head_count) for hop in hops]
    parts = [
        pl.ds(pl.multiple_of(target * block_rows, block_rows), block_rows) for target in targets
    ]

    def hand_over(turn, new_peak, result):
        target = targets[turn]
        rows_f32[turn % 2] = result[:, :LANES] / result[:, LANES:]
        for member in range(group):
            part = rows_f32[turn % 2, pl.ds(member, block_rows // group, stride=group), :]
            outgoing[target, :, member * LANES : (member + 1) * LANES] = part.astype(jnp.bfloat16)
        if hops[turn] > 0:
            send_out(target).start()
        else:
            keep_out().start()

    attend_all(parts, (2 + list_length - early) * LANES, lambda turn: {}, False, hand_over)

    send_prev().wait_send()

    @pl.loop(0, (steps - 1) * ITEMS)
    def _(tick):
        step = tick // ITEMS
        item = tick % ITEMS
        send_up(at(z - step, core), item, step).wait_send()
        send_down(at(z + step, core), item, step).wait_send()
        send_side(at(z - step, core), item).wait_send()

        @pl.when(step > 0)
        def _():
            send_side(at(z + step, core), item).wait_send()

    for item in range(ITEMS // 2):
        send_up(at(z - steps + 1, core), item, steps - 1, True).wait_send()
        send_down(at(z + steps - 1, core), item + ITEMS // 2, steps - 1, True).wait_send()

    @pl.loop(0, ITEMS)
    def _(item):
        for step in (1 - steps, steps - 1):
            send_side(at(z + step, core), item).wait_send()
        far_copy(core, item).wait_send()

    keep_out().wait()

    @pl.loop(1, head_count)
    def _(hop):
        peer = lax.rem(head + hop, head_count)
        send_out(peer).wait_send()
        pltpu.make_async_remote_copy(
            src_ref=outgoing.at[peer],
            dst_ref=o_ref.at[:, pl.ds(pl.multiple_of(peer * group * LANES, LANES), group * LANES)],
            send_sem=out_send.at[peer],
            recv_sem=out_recv.at[peer],
            device_id=device(z, core, span, peer),
            device_id_type=MESH,
        ).wait_recv()


def local(query, new_keys, new_values, memory_keys, memory_values, retrieved):
    _, length, _, group, width = query.shape
    units, unit_length = memory_keys.shape[0], memory_keys.shape[1]
    mem_count = lax.axis_size("mem")
    head_count = lax.axis_size("head")
    span_count = lax.axis_size("span")
    list_length = retrieved.shape[2]
    ring = mem_count // 2
    steps = ring // 2
    rows = length * group
    tiles = 2 + max(list_length, 2 * SLOTS)
    scale = math.log2(math.e) / math.sqrt(width)
    sizes = (mem_count, head_count, span_count, units, list_length, group, scale)
    anywhere = pl.BlockSpec(memory_space=pl.ANY)
    dma = pltpu.SemaphoreType.DMA
    out = pl.pallas_call(
        functools.partial(kernel, sizes),
        out_shape=jax.ShapeDtypeStruct(
            (length // head_count, head_count * group * width), jnp.bfloat16
        ),
        in_specs=[anywhere] * 6,
        out_specs=anywhere,
        scratch_shapes=[
            pltpu.VMEM((rows, width), jnp.bfloat16),
            pltpu.VMEM((units, unit_length, width), jnp.bfloat16),
            pltpu.VMEM((units, unit_length, width), jnp.bfloat16),
            pltpu.VMEM((mem_count, 2, ITEMS, unit_length, width), jnp.bfloat16),
            pltpu.VMEM((2, 2, ITEMS, unit_length, width), jnp.bfloat16),
            pltpu.VMEM((2, length, width), jnp.bfloat16),
            pltpu.VMEM((rows, LANES), jnp.float32),
            pltpu.VMEM((rows, 2 * LANES), jnp.float32),
            pltpu.VMEM((2, rows // head_count, width), jnp.float32),
            pltpu.VMEM((head_count, length // head_count, group * width), jnp.bfloat16),
            pltpu.VMEM((tiles * unit_length, width), jnp.bfloat16),
            pltpu.VMEM((tiles * unit_length, 2 * width), jnp.bfloat16),
            pltpu.VMEM((unit_length, width), jnp.bfloat16),
            pltpu.SMEM((list_length,), jnp.int32),
            pltpu.SMEM((1, list_length), jnp.int32),
            dma((6,)),
            dma((mem_count, ITEMS)),
            dma((2, ITEMS)),
            dma((ring, ITEMS)),
            dma((ITEMS,)),
            dma((steps, ITEMS)),
            dma((steps, ITEMS)),
            dma((2,)),
            dma((head_count,)),
            dma((head_count,)),
            pltpu.SemaphoreType.REGULAR((2, max(1, head_count // 2 - 1))),
        ],
        compiler_params=pltpu.CompilerParams(
            collective_id=0, has_side_effects=True, vmem_limit_bytes=62 * 1024 * 1024
        ),
    )(
        query.reshape(rows, width),
        new_keys.reshape(length, width),
        new_values.reshape(length, width),
        memory_keys.reshape(units, unit_length, width),
        memory_values.reshape(units, unit_length, width),
        retrieved.reshape(1, list_length),
    )
    return out[None]


def solution(mesh):
    return jax.shard_map(
        local,
        mesh=mesh,
        in_specs=(
            P("span", "mem", "head", None, None),
            P("span", "mem", "head", None),
            P("span", "mem", "head", None),
            P("mem", None, "head", None),
            P("mem", None, "head", None),
            P("span", "head", None),
        ),
        out_specs=P("span", ("mem", "head"), None),
        check_vma=False,
    )
```

```python
import functools
import math

import jax
import jax.numpy as jnp
from jax import lax
from jax.experimental import pallas as pl
from jax.experimental.pallas import tpu as pltpu
from jax.sharding import PartitionSpec as P

MESH = pl.DeviceIdType.MESH
LANES = 128
SLOTS = 3
ITEMS = 1 + SLOTS
ROWS = 256
HUGE = 1e30


def kernel(
    sizes,
    q_hbm,
    nk_hbm,
    nv_hbm,
    mk_hbm,
    mv_hbm,
    lists_hbm,
    o_ref,
    q_v,
    mk_v,
    mv_v,
    buf,
    far,
    prev,
    peak,
    accum,
    rows_f32,
    outgoing,
    key_tiles,
    value_tiles,
    filler,
    table,
    lists,
    local_sem,
    recv_sem,
    far_sem,
    side_sem,
    far_side_sem,
    up_sem,
    down_sem,
    prev_sem,
    out_send,
    out_recv,
    word_sem,
):
    mem_count, head_count, span_count, unit_count, list_length, group, scale = sizes
    ring = mem_count // 2
    steps = ring // 2
    row_count = q_v.shape[0]
    block_rows = row_count // head_count
    mem = lax.axis_index("mem")
    head = lax.axis_index("head")
    span = lax.axis_index("span")
    z = mem // 2
    core = mem % 2

    def device(z_at, core_at, span_at, head_at=None):
        return {
            "mem": lax.rem(z_at + ring, ring) * 2 + core_at,
            "head": head if head_at is None else head_at,
            "span": lax.rem(span_at + span_count, span_count),
        }

    loads = [
        pltpu.make_async_copy(nk_hbm, buf.at[mem, 0, 0], local_sem.at[0]),
        pltpu.make_async_copy(nv_hbm, buf.at[mem, 1, 0], local_sem.at[1]),
        pltpu.make_async_copy(mk_hbm, mk_v, local_sem.at[2]),
        pltpu.make_async_copy(mv_hbm, mv_v, local_sem.at[3]),
        pltpu.make_async_copy(q_hbm, q_v, local_sem.at[4]),
        pltpu.make_async_copy(lists_hbm, lists, local_sem.at[5]),
    ]
    loads[0].start()
    loads[1].start()
    loads[5].start()

    barrier = pltpu.get_barrier_semaphore()
    near = [
        (dz, 0, dx)
        for dz, dx in ((1, 0), (-1, 0), (0, 1), (0, -1), (1, 1), (-1, -1), (1, -1), (-1, 1))
    ]
    near += [(0, 1, 0), (0, 1, 1), (0, 1, -1)]
    for dz, dc, dx in near:
        pl.semaphore_signal(
            barrier,
            inc=1,
            device_id=device(z + dz, core if dc == 0 else 1 - core, span + dx),
            device_id_type=MESH,
        )
    for load in loads[2:5]:
        load.start()
    beyond = [lax.rem(head + hop, head_count) for hop in (1, head_count - 1)]
    for head_at in beyond:
        pl.semaphore_signal(
            barrier, inc=1, device_id=device(z, core, span, head_at), device_id_type=MESH
        )

    rounds = head_count // 2 - 1

    def tell(turn):
        for way, head_at in enumerate(beyond):
            pl.semaphore_signal(
                word_sem.at[way, turn],
                inc=1,
                device_id=device(z, core, span, head_at),
                device_id_type=MESH,
            )

    def hear(turn):
        for way in range(2):
            pl.semaphore_wait(word_sem.at[way, turn], 1)

    def owner(entry):
        return lists[0, entry] // unit_count

    def at(z_at, core_at):
        return lax.rem(z_at + ring, ring) * 2 + core_at

    far_z = lax.rem(z + steps, ring)

    def transfer(source, item, send_sem, target, last=False):
        if last:
            landing, landed = far.at[core, :, item], far_sem.at[core, item]
        else:
            landing, landed = buf.at[source, :, item], recv_sem.at[source, item]
        return pltpu.make_async_remote_copy(
            src_ref=buf.at[source, :, item],
            dst_ref=landing,
            send_sem=send_sem,
            recv_sem=landed,
            device_id=target,
            device_id_type=MESH,
        )

    def send_up(source, item, step, last=False):
        shift = jnp.where((z == ring - 1) & (item == 0), 1, 0)
        target = device(z + 1, core, span + shift)
        return transfer(source, item, up_sem.at[step, item], target, last)

    def send_down(source, item, step, last=False):
        first = jnp.where(z > 0, 1, 0)
        later = jnp.where(z > 0, 0, -1)
        shift = jnp.where(item == 0, jnp.where(step == 0, first, later), 0)
        target = device(z - 1, core, span + shift)
        return transfer(source, item, down_sem.at[step, item], target, last)

    def send_side(source, item):
        own = source == mem
        shift = jnp.where(own & (item == 0), core, 0)
        return transfer(
            source, item, side_sem.at[source // 2, item], device(z, 1 - core, span + shift)
        )

    def far_copy(origin, item):
        return pltpu.make_async_remote_copy(
            src_ref=far.at[origin, :, item],
            dst_ref=far.at[origin, :, item],
            send_sem=far_side_sem.at[item],
            recv_sem=far_sem.at[origin, item],
            device_id=device(z, 1 - core, span),
            device_id_type=MESH,
        )

    def send_prev():
        return pltpu.make_async_remote_copy(
            src_ref=buf.at[mem, :, 0],
            dst_ref=prev,
            send_sem=prev_sem.at[0],
            recv_sem=prev_sem.at[1],
            device_id=device(z, core, span + 1),
            device_id_type=MESH,
        )

    def wait_item(source, item):
        send_side(source, item).wait_recv()

    def send_own(item):
        send_up(mem, item, 0).start()
        send_down(mem, item, 0).start()
        send_side(mem, item).start()

    loads[5].wait()
    owners = [owner(entry) for entry in range(list_length)]
    picks = [jnp.int32(0)] * SLOTS
    rank = jnp.int32(0)
    for entry in range(list_length):
        here = owners[entry] == mem
        for slot in range(SLOTS):
            picks[slot] = jnp.where(
                here & (rank == slot), lists[0, entry] % unit_count, picks[slot]
            )
        rank = rank + here.astype(jnp.int32)
    loads[0].wait()
    loads[1].wait()
    pl.semaphore_wait(barrier, len(near) + 2)
    send_own(0)
    send_prev().start()
    loads[2].wait()
    loads[3].wait()
    for slot in range(SLOTS):
        buf[mem, 0, 1 + slot] = mk_v[picks[slot]]
        buf[mem, 1, 1 + slot] = mv_v[picks[slot]]
    filler[...] = jnp.broadcast_to(buf[mem, 0, 0, 0:1, :], filler.shape)

    ranks = []
    for entry in range(list_length):
        same = jnp.int32(0)
        for earlier in range(entry):
            same = same + (owners[earlier] == owners[entry]).astype(jnp.int32)
        ranks.append(same)
    for item in range(1, ITEMS):
        send_own(item)
    if rounds > 0:
        tell(0)
    distant = [(held // 2 == far_z).astype(jnp.int32) for held in owners]
    place_far = jnp.int32(list_length) - sum(distant)
    place_near = jnp.int32(0)
    places = []
    for entry in range(list_length):
        places.append(jnp.where(distant[entry] == 1, place_far, place_near))
        place_far = place_far + distant[entry]
        place_near = place_near + 1 - distant[entry]
    for place in range(list_length):
        code = jnp.int32(0)
        for entry in range(list_length):
            value = owners[entry] * ITEMS + 1 + ranks[entry]
            code = code + jnp.where(places[entry] == place, value, 0)
        table[place] = code
    loads[4].wait()

    def put(tile, keys, values, ones):
        tile = pl.ds(tile * LANES, LANES)
        key_tiles[tile, :] = keys
        value_tiles[tile, :LANES] = values
        value_tiles[tile, LANES:] = ones

    ones = jnp.ones((LANES, LANES), jnp.bfloat16)

    def put_chunk(tile, source, keys, values):
        used = (source < mem) | (span > 0)
        weight = jnp.full((LANES, LANES), jnp.where(used, 1.0, 0.0), jnp.float32)
        put(
            tile,
            jnp.where(used, keys, filler[...]),
            jnp.where(used, values, jnp.bfloat16(0)),
            weight.astype(jnp.bfloat16),
        )

    def put_unit(tile, place, maybe_far):
        held = table[place] // ITEMS
        item = table[place] % ITEMS
        pair = [buf[held, kind, item] for kind in range(2)]
        if maybe_far:
            there = held // 2 == far_z
            pair = [
                jnp.where(there, far[held % 2, kind, item], pair[kind]) for kind in range(2)
            ]
        put(tile, pair[0], pair[1], ones)

    def score(rows, width, masks):
        scores = lax.dot_general(
            q_v[rows, :],
            key_tiles[:width, :],
            (((1,), (1,)), ((), ())),
            preferred_element_type=jnp.float32,
        )
        if masks:
            tiles = [scores[:, t * LANES : (t + 1) * LANES] for t in range(width // LANES)]
            for t, mask in masks.items():
                tiles[t] = jnp.where(mask, tiles[t], -HUGE)
            scores = jnp.concatenate(tiles, axis=1)
        return scores

    def weigh(rows, width, scores, fresh):
        best = jnp.max(scores, axis=1, keepdims=True)
        factor = None
        if fresh:
            new_peak = jnp.broadcast_to(best, (scores.shape[0], LANES))
        else:
            old_peak = peak[rows, :]
            new_peak = jnp.maximum(old_peak, best)
            factor = jnp.exp2((old_peak - new_peak) * scale)
        wide_peak = jnp.concatenate([new_peak] * (width // LANES), axis=1)
        weights = jnp.exp2((scores - wide_peak) * scale)
        return new_peak, factor, weights.astype(jnp.bfloat16)

    def combine(rows, width, weights, factor):
        result = jnp.dot(weights, value_tiles[:width, :], preferred_element_type=jnp.float32)
        if factor is not None:
            result = accum[rows, :] * jnp.concatenate([factor, factor], axis=1) + result
        return result

    def attend_all(blocks, width, masks_of, fresh, finish, prompt=False):
        count = len(blocks)
        scores = score(blocks[0], width, masks_of(0))
        weighed = None
        for index in range(count + 1):
            following = None
            if index + 1 < count:
                following = score(blocks[index + 1], width, masks_of(index + 1))
            done = weighed
            if index < count:
                weighed = weigh(blocks[index], width, scores, fresh)
            if prompt and index < count:
                new_peak, factor, weights = weighed
                finish(index, new_peak, combine(blocks[index], width, weights, factor))
            elif done is not None and not prompt:
                new_peak, factor, weights = done
                finish(index - 1, new_peak, combine(blocks[index - 1], width, weights, factor))
            scores = following

    blocks = [pl.ds(start, ROWS) for start in range(0, row_count, ROWS)]

    def own_masks(index):
        position = (index * ROWS + lax.broadcasted_iota(jnp.int32, (ROWS, LANES), 0)) // group
        column = lax.broadcasted_iota(jnp.int32, (ROWS, LANES), 1)
        return {0: column <= position, 2: (column > position) & (span > 0)}

    def keep(index, new_peak, result):
        peak[blocks[index], :] = new_peak
        accum[blocks[index], :] = result

    beside = at(z, 1 - core)

    def begin():
        put(0, buf[mem, 0, 0], buf[mem, 1, 0], ones)
        wait_item(beside, 0)
        put_chunk(1, beside, buf[beside, 0, 0], buf[beside, 1, 0])
        send_prev().wait_recv()
        put(2, prev[0], prev[1], ones)
        attend_all(blocks, 3 * LANES, own_masks, True, keep)

    def absorb(tiles):
        attend_all(blocks, tiles * LANES, lambda index: {}, False, keep)

    @pl.loop(0, (steps - 1) * ITEMS)
    def _(tick):
        step = tick // ITEMS + 1
        item = tick % ITEMS
        turning = step == steps - 1
        below = at(z - step, core)
        wait_item(below, item)

        @pl.when(jnp.logical_not(turning))
        def _():
            send_up(below, item, step).start()

        @pl.when(turning & (item < ITEMS // 2))
        def _():
            send_up(below, item, step, True).start()

        send_side(below, item).start()
        above = at(z + step, core)
        wait_item(above, item)

        @pl.when(jnp.logical_not(turning))
        def _():
            send_down(above, item, step).start()

        @pl.when(turning & (item >= ITEMS // 2))
        def _():
            send_down(above, item, step, True).start()

        send_side(above, item).start()

        for turn in range(1, rounds):

            @pl.when(tick == turn * ITEMS)
            def _():
                hear(turn - 1)
                tell(turn)

        @pl.when(tick == 1)
        def _():
            begin()

        @pl.when((tick > 1) & (tick % 3 == 0))
        def _():
            reach = tick // 3
            for tile, (distance, core_at) in enumerate(
                ((-reach, core), (reach, core), (-reach, 1 - core), (reach, 1 - core))
            ):
                source = at(z + distance, core_at)
                if tile >= 2:
                    wait_item(source, 0)
                put_chunk(tile, source, buf[source, 0, 0], buf[source, 1, 0])
            absorb(4)

    sure = list_length - 2 * SLOTS
    early = min(3 * list_length // 8, sure) // 2 * 2
    for item in range(1, ITEMS):
        wait_item(beside, item)

    @pl.loop(0, (steps - 1) * (ITEMS - 1))
    def _(tick):
        step = tick // (ITEMS - 1) + 1
        item = tick % (ITEMS - 1) + 1
        wait_item(at(z - step, 1 - core), item)
        wait_item(at(z + step, 1 - core), item)

    def put_early(first, past):
        for place in range(first, past):
            put_unit(place - first, place, False)

    split = min(ITEMS, early)
    put_early(0, split)
    for half in range(2):
        for item in (half, half + ITEMS // 2):
            far_copy(core, item).wait_recv()
            far_copy(core, item).start()
        if half == 0:
            absorb(split)
        elif early > split:
            put_early(split, early)
            absorb(early - split)

    if rounds > 0:
        hear(rounds - 1)
    for place in range(early, sure):
        put_unit(2 + place - early, place, False)
    for item in range(ITEMS):
        far_copy(1 - core, item).wait_recv()

    def send_out(target):
        return pltpu.make_async_remote_copy(
            src_ref=outgoing.at[target],
            dst_ref=o_ref.at[:, pl.ds(pl.multiple_of(head * group * LANES, LANES), group * LANES)],
            send_sem=out_send.at[target],
            recv_sem=out_recv.at[head],
            device_id=device(z, core, span, target),
            device_id_type=MESH,
        )

    def keep_out():
        return pltpu.make_async_copy(
            outgoing.at[head],
            o_ref.at[:, pl.ds(pl.multiple_of(head * group * LANES, LANES), group * LANES)],
            out_send.at[head],
        )

    for origin in range(2):
        put_chunk(origin, far_z * 2 + origin, far[origin, 0, 0], far[origin, 1, 0])
    for place in range(sure, list_length):
        put_unit(2 + place - early, place, True)
    half = head_count // 2
    hops = [half]
    for hop in range(1, half):
        hops += [half - hop, half + hop]
    hops += [0]
    targets = [lax.rem(head + hop, head_count) for hop in hops]
    parts = [
        pl.ds(pl.multiple_of(target * block_rows, block_rows), block_rows) for target in targets
    ]

    def hand_over(turn, new_peak, result):
        target = targets[turn]
        rows_f32[turn % 2] = result[:, :LANES] / result[:, LANES:]
        for member in range(group):
            part = rows_f32[turn % 2, pl.ds(member, block_rows // group, stride=group), :]
            outgoing[target, :, member * LANES : (member + 1) * LANES] = part.astype(jnp.bfloat16)
        if hops[turn] > 0:
            send_out(target).start()
        else:
            keep_out().start()

    attend_all(parts, (2 + list_length - early) * LANES, lambda turn: {}, False, hand_over, True)

    send_prev().wait_send()

    @pl.loop(0, (steps - 1) * ITEMS)
    def _(tick):
        step = tick // ITEMS
        item = tick % ITEMS
        send_up(at(z - step, core), item, step).wait_send()
        send_down(at(z + step, core), item, step).wait_send()
        send_side(at(z - step, core), item).wait_send()

        @pl.when(step > 0)
        def _():
            send_side(at(z + step, core), item).wait_send()

    for item in range(ITEMS // 2):
        send_up(at(z - steps + 1, core), item, steps - 1, True).wait_send()
        send_down(at(z + steps - 1, core), item + ITEMS // 2, steps - 1, True).wait_send()

    @pl.loop(0, ITEMS)
    def _(item):
        for step in (1 - steps, steps - 1):
            send_side(at(z + step, core), item).wait_send()
        far_copy(core, item).wait_send()

    keep_out().wait()

    @pl.loop(1, head_count)
    def _(hop):
        peer = lax.rem(head + hop, head_count)
        send_out(peer).wait_send()
        pltpu.make_async_remote_copy(
            src_ref=outgoing.at[peer],
            dst_ref=o_ref.at[:, pl.ds(pl.multiple_of(peer * group * LANES, LANES), group * LANES)],
            send_sem=out_send.at[peer],
            recv_sem=out_recv.at[peer],
            device_id=device(z, core, span, peer),
            device_id_type=MESH,
        ).wait_recv()


def local(query, new_keys, new_values, memory_keys, memory_values, retrieved):
    _, length, _, group, width = query.shape
    units, unit_length = memory_keys.shape[0], memory_keys.shape[1]
    mem_count = lax.axis_size("mem")
    head_count = lax.axis_size("head")
    span_count = lax.axis_size("span")
    list_length = retrieved.shape[2]
    ring = mem_count // 2
    steps = ring // 2
    rows = length * group
    tiles = 2 + max(list_length, 2 * SLOTS)
    scale = math.log2(math.e) / math.sqrt(width)
    sizes = (mem_count, head_count, span_count, units, list_length, group, scale)
    anywhere = pl.BlockSpec(memory_space=pl.ANY)
    dma = pltpu.SemaphoreType.DMA
    out = pl.pallas_call(
        functools.partial(kernel, sizes),
        out_shape=jax.ShapeDtypeStruct(
            (length // head_count, head_count * group * width), jnp.bfloat16
        ),
        in_specs=[anywhere] * 6,
        out_specs=anywhere,
        scratch_shapes=[
            pltpu.VMEM((rows, width), jnp.bfloat16),
            pltpu.VMEM((units, unit_length, width), jnp.bfloat16),
            pltpu.VMEM((units, unit_length, width), jnp.bfloat16),
            pltpu.VMEM((mem_count, 2, ITEMS, unit_length, width), jnp.bfloat16),
            pltpu.VMEM((2, 2, ITEMS, unit_length, width), jnp.bfloat16),
            pltpu.VMEM((2, length, width), jnp.bfloat16),
            pltpu.VMEM((rows, LANES), jnp.float32),
            pltpu.VMEM((rows, 2 * LANES), jnp.float32),
            pltpu.VMEM((2, rows // head_count, width), jnp.float32),
            pltpu.VMEM((head_count, length // head_count, group * width), jnp.bfloat16),
            pltpu.VMEM((tiles * unit_length, width), jnp.bfloat16),
            pltpu.VMEM((tiles * unit_length, 2 * width), jnp.bfloat16),
            pltpu.VMEM((unit_length, width), jnp.bfloat16),
            pltpu.SMEM((list_length,), jnp.int32),
            pltpu.SMEM((1, list_length), jnp.int32),
            dma((6,)),
            dma((mem_count, ITEMS)),
            dma((2, ITEMS)),
            dma((ring, ITEMS)),
            dma((ITEMS,)),
            dma((steps, ITEMS)),
            dma((steps, ITEMS)),
            dma((2,)),
            dma((head_count,)),
            dma((head_count,)),
            pltpu.SemaphoreType.REGULAR((2, max(1, head_count // 2 - 1))),
        ],
        compiler_params=pltpu.CompilerParams(
            collective_id=0, has_side_effects=True, vmem_limit_bytes=62 * 1024 * 1024
        ),
    )(
        query.reshape(rows, width),
        new_keys.reshape(length, width),
        new_values.reshape(length, width),
        memory_keys.reshape(units, unit_length, width),
        memory_values.reshape(units, unit_length, width),
        retrieved.reshape(1, list_length),
    )
    return out[None]


def solution(mesh):
    return jax.shard_map(
        local,
        mesh=mesh,
        in_specs=(
            P("span", "mem", "head", None, None),
            P("span", "mem", "head", None),
            P("span", "mem", "head", None),
            P("mem", None, "head", None),
            P("mem", None, "head", None),
            P("span", "head", None),
        ),
        out_specs=P("span", ("mem", "head"), None),
        check_vma=False,
    )
```
